128 devices in a mesh: dp: 64 (over x, z, y), rep: 2 (over core).
Axes of the slice: x: 4, y: 4, z: 4, core: 2. Of those that a mesh axis runs over, the one named last changes fastest.
Arguments:
- pooled: bfloat16 [16, 128, 32768], P(None, ('dp', 'rep')), may hold values from -6 to 6
- slot_of_block: int32 [128], replicated, may hold values from 0 to 127, each once
- dense_part: bfloat16 [128, 32768], P(None, ('dp', 'rep')), may hold values from -6 to 6
- labels: int32 [32768], P(('dp', 'rep')), may hold values 0 or 1
- sample_weight: float32 [32768], P(('dp', 'rep')), may hold values from 0.5 to 18, as said below
- proj_wide: bfloat16 [6, 256, 128], replicated, may hold values from -0.375 to 0.375
- proj_mid: bfloat16 [4, 64, 128], replicated, may hold values from -0.75 to 0.75
- proj_narrow: bfloat16 [16, 16, 128], replicated, may hold values from -1.5 to 1.5
- cross_in: bfloat16 [2, 3456, 256], replicated, may hold values from -0.109375 to 0.109375
- cross_out: bfloat16 [2, 256, 3456], replicated, may hold values from -0.375 to 0.375
- cross_bias: float32 [2, 3456], replicated, may hold values from -3 to 3
- head_weight: float32 [3456], replicated, may hold values from -0.24 to 0.24
Outputs:
- pooled_grad: float32 [16, 128, 32768], P(None, ('dp', 'rep'))
- grad_cross_in: float32 [2, 3456, 256], P(None, ('dp', 'rep'))
- grad_cross_out: float32 [2, 256, 3456], P(None, None, ('dp', 'rep'))
- grad_bias: float32 [2, 3456], P(None, ('dp', 'rep'))
The draws below stay inside these ranges and needn't reach their ends.
Inputs may be any that keep to these rules, and one draw needn't show every extreme that they name: `slot_of_block`: each number of 0 to 127 appears once. `sample_weight`: positive.
All inputs are finite; a program needn't handle non-finite values. No bound on the sum of `labels` on one device may be relied on, other than what follows from the above.
Results may differ from the reference program's by a relative error of at most 0.014.
Values may be sent and summed in bfloat16 or wider, within the bound.
A program may use at most 128 MiB of HBM per device.

```python
import math
import jax
import jax.numpy as jnp
from jax import lax

BLOCK_WIDTH = 16
WIDE_TABLES = 6
MID_TABLES = 4
NARROW_TABLES = 16
WIDE_WIDTH = 256
MID_WIDTH = 64
NARROW_WIDTH = 16
PROJECTED = 128
CROSS_RANK = 256
LAYERS = 2
ROWS_DEV = 256
BLOCKS = 128
CROSS_WIDTH = 3456
BATCH_ROWS = 32768
N_DP = 64
N_REP = 2


def draw_sample_weight(key, part):
    base_weight = jnp.exp(jax.random.uniform(key, (BATCH_ROWS,), jnp.float32, math.log(0.5), math.log(2.0)))
    owner_index = (jnp.arange(BATCH_ROWS) // ROWS_DEV).astype(jnp.float32)
    fraction = owner_index / max(N_DP * N_REP - 1, 1)
    factor = 1.0 + 2.0 * fraction
    return (base_weight * factor).astype(jnp.float32)


def place_ends(entries, key, smallest, high):
    place = [jax.random.randint(jax.random.fold_in(key, axis), (), 0, length) for axis, length in enumerate(entries.shape)]
    main_axis = entries.shape.index(max(entries.shape))
    next_to = place[:main_axis] + [(place[main_axis] + 1) % entries.shape[main_axis]] + place[main_axis + 1:]
    return entries.at[tuple(place)].set(smallest).at[tuple(next_to)].set(high)


def shard_levels(own_key, shape, cuts, low, high):
    factor_of = 1.0
    for axis_at, blocks in cuts:
        heights = jax.random.uniform(jax.random.fold_in(jax.random.fold_in(own_key, 6), axis_at), (blocks,), jnp.float32, low / len(cuts), high / len(cuts))
        factor_of = factor_of * jnp.repeat(jnp.exp(heights), shape[axis_at] // blocks).reshape((-1,) + (1,) * (len(shape) - 1 - axis_at))
    return factor_of


def scatter_about(key, shape, deviation, reach, cuts=(), kind=jnp.bfloat16):
    array = deviation * jax.random.normal(key, shape, jnp.float32)
    if cuts:
        array = array * shard_levels(key, shape, cuts, -0.22, 0.18)
    return jnp.clip(array, -reach, reach).astype(kind)


def setup_inputs(seed: int = 0) -> dict:
    key_list = jax.random.split(jax.random.key(seed), 13)
    return {
        "pooled": scatter_about(key_list[0], (BLOCK_WIDTH, BLOCKS, BATCH_ROWS), 1.0, 6.0, ((1, 128),)),
        "slot_of_block": jax.random.permutation(key_list[1], BLOCKS).astype(jnp.int32),
        "dense_part": scatter_about(key_list[2], (PROJECTED, BATCH_ROWS), 1.0, 6.0, ((1, 128),)),
        "labels": place_ends((jax.random.randint(key_list[3], (BATCH_ROWS,), 0, 2) < 1).astype(jnp.int32), jax.random.fold_in(key_list[3], 1), 0, 1),
        "sample_weight": draw_sample_weight(jax.random.fold_in(key_list[12], 71), 0),
        "proj_wide": scatter_about(key_list[5], (WIDE_TABLES, WIDE_WIDTH, PROJECTED), WIDE_WIDTH ** -0.5, 0.375),
        "proj_mid": scatter_about(key_list[6], (MID_TABLES, MID_WIDTH, PROJECTED), MID_WIDTH ** -0.5, 0.75),
        "proj_narrow": scatter_about(key_list[7], (NARROW_TABLES, NARROW_WIDTH, PROJECTED), NARROW_WIDTH ** -0.5, 1.5),
        "cross_in": scatter_about(key_list[8], (LAYERS, CROSS_WIDTH, CROSS_RANK), CROSS_WIDTH ** -0.5, 0.109375),
        "cross_out": scatter_about(key_list[9], (LAYERS, CROSS_RANK, CROSS_WIDTH), CROSS_RANK ** -0.5, 0.375),
        "cross_bias": scatter_about(key_list[10], (LAYERS, CROSS_WIDTH), 0.5, 3.0, (), jnp.float32),
        "head_weight": scatter_about(key_list[11], (CROSS_WIDTH,), 0.04, 0.24, (), jnp.float32),
    }


def table_layout():
    first_end = WIDE_TABLES * (WIDE_WIDTH // BLOCK_WIDTH)
    second_end = first_end + MID_TABLES * (MID_WIDTH // BLOCK_WIDTH)
    return ((0, first_end, WIDE_TABLES, WIDE_WIDTH), (first_end, second_end, MID_TABLES, MID_WIDTH), (second_end, BLOCKS, NARROW_TABLES, NARROW_WIDTH))


def project_tables(logical, proj_tables):
    row_count = logical.shape[2]
    outputs = []
    for layout, proj_table in zip(table_layout(), proj_tables):
        block_start, block_end, table_count, table_width = layout
        pieces = logical[:, block_start:block_end].reshape(BLOCK_WIDTH, table_count, table_width // BLOCK_WIDTH, row_count)
        matrix = proj_table.reshape(table_count, table_width // BLOCK_WIDTH, BLOCK_WIDTH, PROJECTED)
        result = jnp.einsum('tkco,ctkr->tor', matrix.astype(jnp.float32), pieces.astype(jnp.float32))
        outputs.append(result.reshape(table_count * PROJECTED, row_count))
    return jnp.concatenate(outputs, 0)


def project_back(proj_grad, proj_tables):
    row_count = proj_grad.shape[1]
    outputs = []
    offset = 0
    for layout, proj_table in zip(table_layout(), proj_tables):
        block_start, block_end, table_count, table_width = layout
        piece = proj_grad[offset:offset + table_count * PROJECTED].reshape(table_count, PROJECTED, row_count)
        offset = offset + table_count * PROJECTED
        matrix = proj_table.reshape(table_count, table_width // BLOCK_WIDTH, BLOCK_WIDTH, PROJECTED)
        result = jnp.einsum('tkco,tor->ctkr', matrix.astype(jnp.float32), piece.astype(jnp.float32))
        outputs.append(result.reshape(BLOCK_WIDTH, block_end - block_start, row_count))
    return jnp.concatenate(outputs, 1)


def block_step(slots, dense_part, labels, sample_weight, slot_of_block, proj_tables, cross_in, cross_out, cross_bias, head_weight):
    logical = jnp.take(slots, slot_of_block, axis=1)
    projected = project_tables(logical, proj_tables)
    start = jnp.concatenate([dense_part.astype(jnp.float32), projected], 0).astype(jnp.bfloat16)
    start_full = start.astype(jnp.float32)
    layer_inputs = [start]
    hidden_list = []
    gate_list = []
    current = start
    for layer in range(LAYERS):
        hidden = jnp.dot(cross_in[layer].T, current, preferred_element_type=jnp.float32).astype(jnp.bfloat16)
        gate = jnp.dot(cross_out[layer].T, hidden, preferred_element_type=jnp.float32) + cross_bias[layer][:, None]
        current = (start_full * gate + current.astype(jnp.float32)).astype(jnp.bfloat16)
        hidden_list.append(hidden)
        gate_list.append(gate)
        layer_inputs.append(current)
    logit = jnp.dot(head_weight, current.astype(jnp.float32), precision=lax.Precision.HIGHEST)
    signal = sample_weight * (jax.nn.sigmoid(logit) - labels.astype(jnp.float32))
    upstream = head_weight[:, None] * signal[None, :]
    start_grad = jnp.zeros(start_full.shape, jnp.float32)
    in_terms = [None] * LAYERS
    out_terms = [None] * LAYERS
    bias_terms = [None] * LAYERS
    for layer in reversed(range(LAYERS)):
        gate_grad = start_full * upstream
        bias_terms[layer] = jnp.sum(gate_grad, axis=1)
        gate_low = gate_grad.astype(jnp.bfloat16)
        out_terms[layer] = jnp.dot(hidden_list[layer], gate_low.T, preferred_element_type=jnp.float32)
        hidden_grad = jnp.dot(cross_out[layer], gate_low, preferred_element_type=jnp.float32).astype(jnp.bfloat16)
        in_terms[layer] = jnp.dot(layer_inputs[layer], hidden_grad.T, preferred_element_type=jnp.float32)
        start_grad = start_grad + gate_list[layer] * upstream
        upstream = upstream + jnp.dot(cross_in[layer], hidden_grad, preferred_element_type=jnp.float32)
    start_grad = start_grad + upstream
    proj_grad = start_grad[PROJECTED:].astype(jnp.bfloat16)
    logical_grad = project_back(proj_grad, proj_tables)
    slot_grad = jnp.zeros(logical_grad.shape, jnp.float32).at[:, slot_of_block, :].set(logical_grad)
    return slot_grad, jnp.stack(in_terms), jnp.stack(out_terms), jnp.stack(bias_terms)


def reference(pooled, slot_of_block, dense_part, labels, sample_weight, proj_wide, proj_mid, proj_narrow, cross_in, cross_out, cross_bias, head_weight):
    total = jnp.sum(sample_weight)
    scale = BATCH_ROWS / total
    proj_tables = (proj_wide, proj_mid, proj_narrow)
    block_count = N_DP * N_REP

    def step(carry, index):
        row_start = (index * ROWS_DEV).astype(jnp.int32)
        slots = lax.dynamic_slice_in_dim(pooled, row_start, ROWS_DEV, 2)
        dense_rows = lax.dynamic_slice_in_dim(dense_part, row_start, ROWS_DEV, 1)
        label_rows = lax.dynamic_slice_in_dim(labels, row_start, ROWS_DEV, 0)
        weight_rows = lax.dynamic_slice_in_dim(sample_weight, row_start, ROWS_DEV, 0)
        slot_grad, in_term, out_term, bias_term = block_step(slots, dense_rows, label_rows, weight_rows, slot_of_block, proj_tables, cross_in, cross_out, cross_bias, head_weight)
        return (carry[0] + in_term, carry[1] + out_term, carry[2] + bias_term), slot_grad

    initial = (jnp.zeros((LAYERS, CROSS_WIDTH, CROSS_RANK), jnp.float32), jnp.zeros((LAYERS, CROSS_RANK, CROSS_WIDTH), jnp.float32), jnp.zeros((LAYERS, CROSS_WIDTH), jnp.float32))
    sums, stacked = lax.scan(step, initial, jnp.arange(block_count, dtype=jnp.int32))
    pooled_grad = jnp.moveaxis(stacked, 0, 2).reshape(BLOCK_WIDTH, BLOCKS, BATCH_ROWS) * scale
    return (pooled_grad, sums[0] * scale, sums[1] * scale, sums[2] * scale)
```

```python
import jax
import jax.numpy as jnp
from jax import lax
from jax.experimental import pallas as pl
from jax.experimental.pallas import tpu as pltpu
from jax.sharding import Mesh
from jax.sharding import PartitionSpec as P

BLOCK_WIDTH = 16
BLOCKS = 128
DP_REP = ("dp_0", "dp_1", "dp_2", "rep")
AXES = DP_REP
MESH = pl.DeviceIdType.MESH
DEVICES = 128
ROWS = 256
VM = pltpu.VMEM
PARTS = ((0, 96, (0, 1, 2)), (96, 176, (1, 2, 0)), (176, 256, (2, 0, 1)))
OWNED = 256


def place():
    return tuple(lax.axis_index(a) for a in AXES)


def flat(at):
    return ((at[0] * 4 + at[1]) * 4 + at[2]) * 2 + at[3]


def shifted(at, step):
    return tuple((a + (step // s) % n) % n for a, s, n in zip(at, (32, 8, 2, 1), (4, 4, 4, 2)))


def exchange_kernel(x_ref, w_ref, o_ref, t_ref, send_sem, recv_sem, tsend_sem, trecv_sem, local_sem):
    at = place()
    me = flat(at)
    own = pltpu.make_async_copy(x_ref.at[:, pl.ds(pl.multiple_of(me * ROWS, ROWS), ROWS)], o_ref.at[me], local_sem)
    own.start()

    def send(k, carry):
        to = shifted(at, (k * 37) % DEVICES)
        there = flat(to)
        pltpu.make_async_remote_copy(
            src_ref=x_ref.at[:, pl.ds(pl.multiple_of(there * ROWS, ROWS), ROWS)],
            dst_ref=o_ref.at[me], send_sem=send_sem, recv_sem=recv_sem, device_id=to, device_id_type=MESH,
        ).start()
        pltpu.make_async_remote_copy(
            src_ref=w_ref, dst_ref=t_ref.at[me], send_sem=tsend_sem, recv_sem=trecv_sem,
            device_id=to, device_id_type=MESH,
        ).start()
        return carry

    lax.fori_loop(1, DEVICES, send, 0)
    t_ref[me] = w_ref[...]
    own.wait()
    most = o_ref.at[pl.ds(0, DEVICES - 1)]
    small = t_ref.at[pl.ds(0, DEVICES - 1)]
    pltpu.make_async_copy(small, small, tsend_sem).wait()
    pltpu.make_async_copy(most, most, send_sem).wait()
    pltpu.make_async_copy(small, small, trecv_sem).wait()
    pltpu.make_async_copy(most, most, recv_sem).wait()


def exchange(pooled, weight_sum):
    any_space = pl.BlockSpec(memory_space=pl.ANY)
    vmem = pl.BlockSpec(memory_space=VM)
    dma = pltpu.SemaphoreType.DMA
    return pl.pallas_call(
        exchange_kernel,
        out_shape=(jax.ShapeDtypeStruct((DEVICES, 16, ROWS), jnp.bfloat16),
                   jax.ShapeDtypeStruct((DEVICES, 1, 128), jnp.float32)),
        in_specs=[any_space, vmem],
        out_specs=(vmem, vmem),
        scratch_shapes=[dma] * 5,
        compiler_params=pltpu.CompilerParams(has_side_effects=True),
        name="exchange",
    )(pooled, weight_sum)


def sub(ref, chosen, tail):
    return ref.at[tuple(chosen.get(d, slice(None)) for d in range(3)) + tail]


def reduce_kernel(g_ref, s_ref, out_ref, back_ref, *scratch):
    core_buf = scratch[0]
    bufs = [scratch[1 + 6 * p: 7 + 6 * p] for p in range(3)]
    (c_send, c_recv, p1_send, p1_recv, p2_send, p2_recv, p3_send, p3_recv,
     a_send, a_recv, local_sem) = scratch[19:]
    at = place()
    me = flat(at)
    core = at[3]
    other = 1 - core
    partner = at[:3] + (other,)
    steps = (2, 1, 3, 0)
    sent = []

    def remote(src, dst, ss, rs, to):
        copy = pltpu.make_async_remote_copy(
            src_ref=src, dst_ref=dst, send_sem=ss, recv_sem=rs, device_id=to, device_id_type=MESH)
        copy.start()
        sent.append(copy)
        return copy

    def moved(d, k):
        return tuple((a + k) % 4 if i == d else a for i, a in enumerate(at[:3])) + (core,)

    core_copies = {}
    for k in range(4):
        for p, (lo, hi, order) in enumerate(PARTS):
            d = order[0]
            j = (at[d] + steps[k]) % 4
            tail = (pl.ds(lo, hi - lo), slice(None))
            core_copies[p, k] = remote(
                sub(g_ref, {d: j}, (other,) + tail), sub(core_buf, {d: j}, tail),
                c_send.at[p, k], c_recv.at[p, k], partner)

    own = pltpu.make_async_copy(s_ref.at[me], back_ref.at[:, pl.ds(pl.multiple_of(me * ROWS, ROWS), ROWS)], local_sem)
    own.start()

    def send(k, carry):
        to = shifted(at, (k * 37) % DEVICES)
        pltpu.make_async_remote_copy(
            src_ref=s_ref.at[flat(to)],
            dst_ref=back_ref.at[:, pl.ds(pl.multiple_of(me * ROWS, ROWS), ROWS)],
            send_sem=a_send, recv_sem=a_recv, device_id=to, device_id_type=MESH).start()
        return carry

    half = DEVICES // 2
    lax.fori_loop(1, half, send, 0)

    def fold(p, k):
        lo, hi, order = PARTS[p]
        d = order[0]
        j = (at[d] + steps[k]) % 4
        core_copies[p, k].wait_recv()
        tail = (pl.ds(lo, hi - lo), slice(None))
        mine = sub(g_ref, {d: j}, (core,) + tail)
        got = sub(core_buf, {d: j}, tail)
        for i in range(4):
            got[i] = got[i] + mine[i]
        return got

    first = [pl.ds(0, 2), pl.ds(2, 2)]
    p1 = {}
    kept = {}
    for p in range(3):
        d = PARTS[p][2][0]
        ra, rb, rp, rm, r2, r3 = bufs[p]
        far = fold(p, 0)
        p1[p, 0] = remote(far.at[first[0]], ra, p1_send.at[p, 0], p1_recv.at[p, 0], moved(d, 1))
        p1[p, 1] = remote(far.at[first[1]], rb, p1_send.at[p, 1], p1_recv.at[p, 1], moved(d, 3))
    for p in range(3):
        d = PARTS[p][2][0]
        ra, rb, rp, rm, r2, r3 = bufs[p]
        up = fold(p, 1)
        kept[p, 1] = up
        p1[p, 2] = remote(up.at[first[1]], rp.at[first[1]], p1_send.at[p, 2], p1_recv.at[p, 2], moved(d, 1))
        down = fold(p, 2)
        kept[p, 2] = down
        p1[p, 3] = remote(down.at[first[0]], rm.at[first[0]], p1_send.at[p, 3], p1_recv.at[p, 3], moved(d, 3))
    for p in range(3):
        kept[p, 3] = fold(p, 3)
    for p in range(3):
        d = PARTS[p][2][0]
        ra, rb, rp, rm, r2, r3 = bufs[p]
        p1[p, 0].wait_recv()
        up = kept[p, 1].at[first[0]]
        up[...] = up[...] + ra[...]
        p1[p, 4] = remote(up, rp.at[first[0]], p1_send.at[p, 4], p1_recv.at[p, 4], moved(d, 1))
        p1[p, 1].wait_recv()
        down = kept[p, 2].at[first[1]]
        down[...] = down[...] + rb[...]
        p1[p, 5] = remote(down, rm.at[first[1]], p1_send.at[p, 5], p1_recv.at[p, 5], moved(d, 3))
    lax.fori_loop(half, DEVICES, send, 0)

    def select(ref, p, chosen):
        d = PARTS[p][2][0]
        dims = [i for i in range(3) if i != d]
        return ref.at[tuple(chosen.get(i, slice(None)) for i in dims)]

    p2 = {}
    for p in range(3):
        lo, hi, (d, e, f) = PARTS[p]
        ra, rb, rp, rm, r2, r3 = bufs[p]
        for i in range(2, 6):
            p1[p, i].wait_recv()
        total = kept[p, 3]
        for i in range(4):
            total[i] = (total[i].astype(jnp.float32) + rp[i].astype(jnp.float32)
                        + rm[i].astype(jnp.float32)).astype(jnp.bfloat16)
        for k in (2, 1, 3):
            p2[p, k] = remote(select(total, p, {e: (at[e] + k) % 4}), r2.at[k - 1],
                              p2_send.at[p, k - 1], p2_recv.at[p, k - 1], moved(e, k))
    p3 = {}
    held = {}
    for p in range(3):
        lo, hi, (d, e, f) = PARTS[p]
        ra, rb, rp, rm, r2, r3 = bufs[p]
        for k in (1, 2, 3):
            p2[p, k].wait_recv()
        mine = select(kept[p, 3], p, {e: at[e]})
        mine[...] = (mine[...].astype(jnp.float32) + r2[0].astype(jnp.float32) + r2[1].astype(jnp.float32)
                     + r2[2].astype(jnp.float32)).astype(jnp.bfloat16)
        held[p] = mine
        for k in (2, 1, 3):
            p3[p, k] = remote(mine.at[(at[f] + k) % 4], r3.at[k - 1],
                              p3_send.at[p, k - 1], p3_recv.at[p, k - 1], moved(f, k))
    for p in range(3):
        lo, hi, (d, e, f) = PARTS[p]
        ra, rb, rp, rm, r2, r3 = bufs[p]
        for k in (1, 2, 3):
            p3[p, k].wait_recv()
        last = held[p].at[at[f]]
        out_ref[pl.ds(lo, hi - lo), :] = (last[...].astype(jnp.float32) + r3[0].astype(jnp.float32)
                                          + r3[1].astype(jnp.float32) + r3[2].astype(jnp.float32))
    own.wait()
    for copy in sent:
        copy.wait_send()
    most = s_ref.at[pl.ds(0, DEVICES - 1)]
    pltpu.make_async_copy(most, most, a_send).wait()
    pltpu.make_async_copy(most, most, a_recv).wait()


def reduce_and_return(grads, slot_grads):
    vmem = pl.BlockSpec(memory_space=VM)
    dma = pltpu.SemaphoreType.DMA
    low = jnp.bfloat16
    buffers = [VM((4, 4, 4, OWNED, 128), low)]
    for lo, hi, _ in PARTS:
        n = hi - lo
        buffers += [VM((2, 4, n, 128), low), VM((2, 4, n, 128), low), VM((4, 4, n, 128), low),
                    VM((4, 4, n, 128), low), VM((3, 4, n, 128), low), VM((3, n, 128), low)]
    return pl.pallas_call(
        reduce_kernel,
        out_shape=(jax.ShapeDtypeStruct((OWNED, 128), jnp.float32),
                   jax.ShapeDtypeStruct((16, DEVICES * ROWS), jnp.bfloat16)),
        in_specs=[vmem, vmem],
        out_specs=(vmem, vmem),
        scratch_shapes=buffers + [dma((3, 4)), dma((3, 4)), dma((3, 6)), dma((3, 6)), dma((3, 3)), dma((3, 3)),
                                  dma((3, 3)), dma((3, 3)), dma, dma, dma],
        compiler_params=pltpu.CompilerParams(has_side_effects=True, vmem_limit_bytes=58 * 1024 * 1024),
        name="reduce_and_return",
    )(grads, slot_grads)


TILE = 432
OWNERS = 16
WIDTH = 3456
SHARE = 27
SLOT = 32


def contract(a, b, da, db):
    return lax.dot_general(a, b, (((da,), (db,)), ((), ())), preferred_element_type=jnp.float32)


def table_rows():
    rows = []
    column = 0
    for which, (count, width) in enumerate(((6, 256), (4, 64), (16, 16))):
        for t in range(count):
            rows.append((which, t, column, width))
            column += width
    return rows


def step_kernel(slot_ref, block_ref, slots_ref, dense_ref, label_ref, weight_ref, wide_ref, mid_ref, narrow_ref,
                in_ref, out_ref, vec_ref, g_ref, sg_ref,
                in_t, out_t, col, cols_ref, start, layer, low0, low1, gate0, gate1, partial, stage, bias_ref,
                owner_mask, place_mask, proj_low):
    low = jnp.bfloat16
    f32 = jnp.float32
    projections = (wide_ref, mid_ref, narrow_ref)

    for l in range(2):
        in_t[l] = in_ref[l].T
        out_t[l] = out_ref[l].T
    for i in range(WIDTH // 128):
        col[pl.ds(i * 128, 128), :] = vec_ref[:, pl.ds(i * 128, 128)].T
    row = lax.broadcasted_iota(jnp.int32, (TILE, 128), 0)
    lane = lax.broadcasted_iota(jnp.int32, (TILE, 128), 1)
    place_mask[...] = jnp.where(row % SHARE == lane, 1.0, 0.0)
    orow = lax.broadcasted_iota(jnp.int32, (OWNERS, TILE), 0)
    olane = lax.broadcasted_iota(jnp.int32, (OWNERS, TILE), 1)
    owner_mask[...] = jnp.where(olane // SHARE == orow, 1.0, 0.0).astype(low)
    for g in range(4):
        stage[g, pl.ds(TILE, 8), :] = jnp.zeros((8, 128), f32)

    def gather(b, carry):
        cols_ref[pl.ds(pl.multiple_of(b * 16, 16), 16), :] = slots_ref[slot_ref[b]]
        return carry

    lax.fori_loop(0, BLOCKS, gather, 0, unroll=8)
    start[pl.ds(0, 128), :] = dense_ref[...]
    for n, (which, t, column, width) in enumerate(table_rows()):
        start[pl.ds(128 + n * 128, 128), :] = contract(
            projections[which][t], cols_ref[pl.ds(column, width), :], 0, 0).astype(low)

    hidden0 = contract(in_t[0], start[...], 1, 0).astype(low)

    def tile(i):
        return pl.ds(pl.multiple_of(i * TILE, 16), TILE)

    def forward0(i, carry):
        at = tile(i)
        gate = contract(out_t[0, at, :], hidden0, 1, 0) + col[at, 0:1]
        gate0[at, :] = gate
        s = start[at, :].astype(f32)
        layer[at, :] = (s * gate + s).astype(low)
        return carry

    lax.fori_loop(0, WIDTH // TILE, forward0, 0)
    hidden1 = contract(in_t[1], layer[...], 1, 0).astype(low)

    def forward1(i, logit):
        at = tile(i)
        gate = contract(out_t[1, at, :], hidden1, 1, 0) + col[at, 1:2]
        gate1[at, :] = gate
        last = (start[at, :].astype(f32) * gate + layer[at, :].astype(f32)).astype(low).astype(f32)
        return logit + jnp.sum((col[at, 2:3] * last).reshape(TILE // 8, 8, ROWS), axis=0)

    logit = lax.fori_loop(0, WIDTH // TILE, forward1, jnp.zeros((8, ROWS), f32))
    logit = jnp.sum(logit, axis=0, keepdims=True)
    signal = weight_ref[...] * (jax.nn.sigmoid(logit) - label_ref[...])

    def keep_bias(l, i, gate_grad):
        sums = jnp.sum(gate_grad, axis=1, keepdims=True)
        spread = (place_mask[...] * sums).astype(low)
        bias_ref[l, pl.ds(pl.multiple_of(i * OWNERS, 16), OWNERS), :] = contract(owner_mask[...], spread, 1, 0)

    def backward1(i, carry):
        at = tile(i)
        gate_grad = start[at, :].astype(f32) * (col[at, 2:3] * signal)
        keep_bias(1, i, gate_grad)
        low1[at, :] = gate_grad.astype(low)
        return carry

    lax.fori_loop(0, WIDTH // TILE, backward1, 0)
    grad1 = contract(out_ref[1], low1[...], 1, 0).astype(low)
    last_row = lax.broadcasted_iota(jnp.int32, (SLOT, 128), 0) == SHARE

    def pack(l, i, in_term, out_term):
        for h in range(2):
            stage[h, pl.ds(0, TILE), :] = in_term[:, h * 128:(h + 1) * 128]
            stage[2 + h, pl.ds(0, TILE), :] = out_term[:, h * 128:(h + 1) * 128]
        for o in range(OWNERS):
            owner = i * OWNERS + o
            for g, group in enumerate((2 * l, 2 * l + 1, 4 + 2 * l, 5 + 2 * l)):
                piece = stage[g, pl.ds(SHARE * o, SLOT), :]
                if g == 0:
                    piece = jnp.where(last_row, bias_ref[l, pl.ds(owner, 1), :], piece)
                g_ref[owner, pl.ds(group * SLOT, SLOT), :] = piece.astype(low)

    def backward0(i, carry):
        at = tile(i)
        pack(1, i, contract(layer[at, :], grad1, 1, 1), contract(low1[at, :], hidden1, 1, 1))
        above = col[at, 2:3] * signal
        upstream = above + contract(in_ref[1, at, :], grad1, 1, 0)
        gate_grad = start[at, :].astype(f32) * upstream
        keep_bias(0, i, gate_grad)
        low0[at, :] = gate_grad.astype(low)
        partial[at, :] = gate1[at, :] * above + gate0[at, :] * upstream + upstream
        return carry

    lax.fori_loop(0, WIDTH // TILE, backward0, 0)
    grad0 = contract(out_ref[0], low0[...], 1, 0).astype(low)

    def finish(i, carry):
        at = tile(i)
        pack(0, i, contract(start[at, :], grad0, 1, 1), contract(low0[at, :], hidden0, 1, 1))
        proj_low[at, :] = (partial[at, :] + contract(in_ref[0, at, :], grad0, 1, 0)).astype(low)
        return carry

    lax.fori_loop(0, WIDTH // TILE, finish, 0)
    for n, (which, t, column, width) in enumerate(table_rows()):
        cols_ref[pl.ds(column, width), :] = contract(
            projections[which][t], proj_low[pl.ds(128 + n * 128, 128), :], 1, 0).astype(low)

    def spread(s, carry):
        sg_ref[s] = cols_ref[pl.ds(pl.multiple_of(block_ref[s] * 16, 16), 16), :]
        return carry

    lax.fori_loop(0, BLOCKS, spread, 0, unroll=8)


def local_step(slot_of_block, block_of_slot, slots, dense, labels, weights, wide, mid, narrow, cross_in, cross_out,
               vectors):
    vmem = pl.BlockSpec(memory_space=VM)
    smem = pl.BlockSpec(memory_space=pltpu.SMEM)
    low, f32 = jnp.bfloat16, jnp.float32
    wide_low = VM((WIDTH, ROWS), low)
    wide_full = VM((WIDTH, ROWS), f32)
    return pl.pallas_call(
        step_kernel,
        out_shape=(jax.ShapeDtypeStruct((DEVICES, OWNED, 128), low),
                   jax.ShapeDtypeStruct((DEVICES, 16, ROWS), low)),
        in_specs=[smem, smem] + [vmem] * 10,
        out_specs=(vmem, vmem),
        scratch_shapes=[VM((2, 256, WIDTH), low), VM((2, WIDTH, 256), low), VM((WIDTH, 8), f32),
                        VM((2048, ROWS), low), wide_low, wide_low, wide_low, wide_low,
                        wide_full, wide_full, wide_full, VM((4, TILE + 8, 128), f32), VM((2, DEVICES, 128), f32),
                        VM((OWNERS, TILE), low), VM((TILE, 128), f32), wide_low],
        compiler_params=pltpu.CompilerParams(vmem_limit_bytes=60 * 1024 * 1024),
        name="local_step",
    )(slot_of_block, block_of_slot, slots, dense, labels, weights, wide, mid, narrow, cross_in, cross_out, vectors)


def body(
    pooled,
    slot_of_block,
    dense_part,
    labels,
    sample_weight,
    proj_wide,
    proj_mid,
    proj_narrow,
    cross_in,
    cross_out,
    cross_bias,
    head_weight,
):
    batch_rows = pooled.shape[2]
    weight_sum = jnp.broadcast_to(jnp.sum(sample_weight), (1, 128))
    slots, weight_sums = exchange(pooled.reshape(BLOCK_WIDTH, batch_rows), weight_sum)
    numbers = jnp.arange(BLOCKS, dtype=jnp.int32)
    block_of_slot = jnp.sum(jnp.where(slot_of_block[None, :] == numbers[:, None], numbers[None, :], 0), 1)
    vectors = jnp.concatenate([cross_bias, head_weight[None], jnp.zeros((5, WIDTH), jnp.float32)], 0)
    grads, slot_grads = local_step(
        slot_of_block,
        block_of_slot,
        slots,
        dense_part,
        labels.astype(jnp.float32)[None],
        sample_weight[None],
        proj_wide,
        proj_mid,
        proj_narrow,
        cross_in,
        cross_out,
        vectors,
    )
    sums, returned = reduce_and_return(grads.reshape(4, 4, 4, 2, OWNED, 128), slot_grads)
    scale = batch_rows / jnp.sum(weight_sums[:, 0, 0])
    sums = sums.reshape(4, 2, SLOT, 128) * scale
    whole = jnp.moveaxis(sums[:, :, :SHARE], 1, 2).reshape(4, SHARE, 256)
    grad_bias = sums[:2, 0, SHARE, :SHARE]
    pooled_grad = (returned.astype(jnp.float32) * scale).reshape(BLOCK_WIDTH, 1, batch_rows)
    return (pooled_grad, whole[:2], jnp.swapaxes(whole[2:], 1, 2), grad_bias)


def solution(mesh):
    finer = Mesh(mesh.devices.reshape(4, 4, 4, mesh.shape["rep"]), ("dp_0", "dp_1", "dp_2", "rep"))
    return jax.shard_map(
        body,
        mesh=finer,
        in_specs=(
            P(None, DP_REP, None),
            P(),
            P(None, DP_REP),
            P(DP_REP),
            P(DP_REP),
            P(),
            P(),
            P(),
            P(),
            P(),
            P(),
            P(),
        ),
        out_specs=(
            P(None, DP_REP, None),
            P(None, DP_REP, None),
            P(None, None, DP_REP),
            P(None, DP_REP),
        ),
        check_vma=False,
    )
```

```python
import jax
import jax.numpy as jnp
from jax import lax
from jax.experimental import pallas as pl
from jax.experimental.pallas import tpu as pltpu
from jax.sharding import Mesh
from jax.sharding import PartitionSpec as P

BLOCK_WIDTH = 16
BLOCKS = 128
DP_REP = ("dp_0", "dp_1", "dp_2", "rep")
AXES = DP_REP
MESH = pl.DeviceIdType.MESH
DEVICES = 128
ROWS = 256
TILE = 432
TILES = 8
OWNERS = 16
WIDTH = 3456
SHARE = 27
SLOT = 32
OWNED = 128
VM = pltpu.VMEM
PARTS = (
    ((0, 32, (0, 1, 2)), (32, 80, (1, 2, 0)), (80, 128, (2, 0, 1))),
    ((0, 48, (0, 1, 2)), (48, 96, (1, 2, 0)), (96, 128, (2, 0, 1))),
)
HALVES = (pl.ds(0, 2), pl.ds(2, 2))


def place():
    return tuple(lax.axis_index(a) for a in AXES)


def flat(at):
    return ((at[0] * 4 + at[1]) * 4 + at[2]) * 2 + at[3]


def shifted(at, step):
    return tuple((a + (step // s) % n) % n for a, s, n in zip(at, (32, 8, 2, 1), (4, 4, 4, 2)))


def columns(device):
    return pl.ds(pl.multiple_of(device * ROWS, ROWS), ROWS)


def contract(a, b, da, db):
    return lax.dot_general(a, b, (((da,), (db,)), ((), ())), preferred_element_type=jnp.float32)


def table_rows():
    rows = []
    column = 0
    for which, (count, width) in enumerate(((6, 256), (4, 64), (16, 16))):
        for t in range(count):
            rows.append((which, t, column, width))
            column += width
    return rows


def sub(ref, chosen, tail):
    return ref.at[tuple(chosen.get(d, slice(None)) for d in range(3)) + tail]


class Reduction:
    def __init__(self, layer, at, grads, core_buf, bufs, sems, remote):
        self.layer, self.at, self.core = layer, at, at[3]
        self.grads, self.core_buf, self.bufs, self.sems = grads, core_buf, bufs, sems
        self.remote = remote
        self.one, self.two, self.three, self.kept = {}, {}, {}, {}

    def moved(self, d, k):
        return tuple((a + k) % 4 if i == d else a for i, a in enumerate(self.at[:3])) + (self.core,)

    def send_tile(self, i):
        there = pl.ds(2 * (i % 2), 2)
        self.remote(
            self.grads.at[i // 2, there, :, 1 - self.core], self.core_buf.at[i // 2, there],
            self.sems["core_send"].at[self.layer], self.sems["core_recv"].at[self.layer],
            self.at[:3] + (1 - self.core,), False)

    def wait_core(self, which):
        pltpu.make_async_copy(self.core_buf, self.core_buf, self.sems[which].at[self.layer]).wait()

    def step(self, which, p, n, src, dst, d, k):
        return self.remote(src, dst, self.sems[which + "_send"].at[self.layer, p, n],
                           self.sems[which + "_recv"].at[self.layer, p, n], self.moved(d, k), True)

    def first(self):
        self.wait_core("core_recv")

        def fold(b, carry):
            x, z = b // 4, b % 4
            for y in range(4):
                self.core_buf[x, z, y] = self.core_buf[x, z, y] + self.grads[x, z, y, self.core]
            return carry

        lax.fori_loop(0, 16, fold, 0)
        for p, (lo, hi, (d, _, _)) in enumerate(PARTS[self.layer]):
            tail = (pl.ds(lo, hi - lo), slice(None))
            for k in range(4):
                self.kept[p, k] = sub(self.core_buf, {d: (self.at[d] + k) % 4}, tail)
            ra, rb = self.bufs[p][:2]
            self.one[p, 0] = self.step("one", p, 0, self.kept[p, 2].at[HALVES[0]], ra, d, 1)
            self.one[p, 1] = self.step("one", p, 1, self.kept[p, 2].at[HALVES[1]], rb, d, 3)
        for p, (lo, hi, (d, _, _)) in enumerate(PARTS[self.layer]):
            rp, rm = self.bufs[p][2:4]
            self.one[p, 2] = self.step(
                "one", p, 2, self.kept[p, 1].at[HALVES[1]], rp.at[HALVES[1]], d, 1)
            self.one[p, 3] = self.step(
                "one", p, 3, self.kept[p, 3].at[HALVES[0]], rm.at[HALVES[0]], d, 3)

    def middle(self):
        for p, (lo, hi, (d, _, _)) in enumerate(PARTS[self.layer]):
            ra, rb, rp, rm = self.bufs[p][:4]
            self.one[p, 0].wait_recv()
            up = self.kept[p, 1].at[HALVES[0]]
            up[...] = up[...] + ra[...]
            self.one[p, 4] = self.step("one", p, 4, up, rp.at[HALVES[0]], d, 1)
            self.one[p, 1].wait_recv()
            down = self.kept[p, 3].at[HALVES[1]]
            down[...] = down[...] + rb[...]
            self.one[p, 5] = self.step("one", p, 5, down, rm.at[HALVES[1]], d, 3)

    def second(self):
        f32 = jnp.float32
        for p, (lo, hi, (d, e, f)) in enumerate(PARTS[self.layer]):
            rp, rm, r2 = self.bufs[p][2:5]
            for n in range(2, 6):
                self.one[p, n].wait_recv()
            total = self.kept[p, 0]
            for i in range(4):
                total[i] = (total[i].astype(f32) + rp[i].astype(f32) + rm[i].astype(f32)).astype(jnp.bfloat16)
            for k in (2, 1, 3):
                self.two[p, k] = self.step(
                    "two", p, k - 1, self.pick(p, {e: (self.at[e] + k) % 4}), r2.at[k - 1], e, k)

    def pick(self, p, chosen):
        d = PARTS[self.layer][p][2][0]
        return self.kept[p, 0].at[tuple(chosen.get(i, slice(None)) for i in range(3) if i != d)]

    def third(self):
        f32 = jnp.float32
        self.held = {}
        for p, (lo, hi, (d, e, f)) in enumerate(PARTS[self.layer]):
            r2, r3 = self.bufs[p][4:6]
            for k in (1, 2, 3):
                self.two[p, k].wait_recv()
            mine = self.pick(p, {e: self.at[e]})
            mine[...] = (mine[...].astype(f32) + r2[0].astype(f32) + r2[1].astype(f32)
                         + r2[2].astype(f32)).astype(jnp.bfloat16)
            self.held[p] = mine
            for k in (2, 1, 3):
                self.three[p, k] = self.step(
                    "three", p, k - 1, mine.at[(self.at[f] + k) % 4], r3.at[k - 1], f, k)

    def last(self, out_ref):
        f32 = jnp.float32
        for p, (lo, hi, (d, e, f)) in enumerate(PARTS[self.layer]):
            r3 = self.bufs[p][5]
            for k in (1, 2, 3):
                self.three[p, k].wait_recv()
            out_ref[self.layer, pl.ds(lo, hi - lo), :] = (
                self.held[p].at[self.at[f]][...].astype(f32) + r3[0].astype(f32) + r3[1].astype(f32)
                + r3[2].astype(f32))


SEMS = (("core_send", (2,)), ("core_recv", (2,)), ("one_send", (2, 3, 6)), ("one_recv", (2, 3, 6)),
        ("two_send", (2, 3, 3)), ("two_recv", (2, 3, 3)), ("three_send", (2, 3, 3)), ("three_recv", (2, 3, 3)),
        ("fwd_send", ()), ("fwd_recv", ()), ("sum_send", ()), ("sum_recv", ()), ("back_send", ()),
        ("back_recv", ()), ("local", (6,)))


def whole_kernel(slot_ref, block_ref, x_ref, dense_ref, label_ref, weight_ref, wide_ref, mid_ref, narrow_ref,
                 in_hbm, out_hbm, bias_in, head_ref, sums_ref, back_ref, total_ref,
                 slots_ref, w_ref, t_ref, in_ref, out_ref, in_t, out_t, vec_ref, col, cols_ref, sg_ref, lg_ref, start, layer,
                 low0, low1, gate0, gate1, stage, bias_ref, owner_mask, place_mask, *rest):
    low = jnp.bfloat16
    f32 = jnp.float32
    projections = (wide_ref, mid_ref, narrow_ref)
    grads, core_bufs, rest = rest[:2], rest[2:4], rest[4:]
    rs_bufs = [[rest[(l * 3 + p) * 6:(l * 3 + p + 1) * 6] for p in range(3)] for l in range(2)]
    sems = {name: sem for (name, _), sem in zip(SEMS, rest[36:])}
    at = place()
    me = flat(at)
    sent = []

    def remote(src, dst, ss, rs, to, keep):
        copy = pltpu.make_async_remote_copy(
            src_ref=src, dst_ref=dst, send_sem=ss, recv_sem=rs, device_id=to, device_id_type=MESH)
        copy.start()
        if keep:
            sent.append(copy)
        return copy

    barrier = pltpu.get_barrier_semaphore()

    def greet(k, carry):
        pl.semaphore_signal(barrier, inc=1, device_id=shifted(at, k), device_id_type=MESH)
        return carry

    lax.fori_loop(1, DEVICES, greet, 0)
    loads = []
    for l in range(2):
        loads.append(pltpu.make_async_copy(in_hbm.at[l], in_ref.at[l], sems["local"].at[l]))
        loads.append(pltpu.make_async_copy(out_hbm.at[l], out_ref.at[l], sems["local"].at[2 + l]))
    for load in loads:
        load.start()
    own = pltpu.make_async_copy(x_ref.at[:, columns(me)], slots_ref.at[me], sems["local"].at[4])
    own.start()
    local_sum = jnp.sum(weight_ref[...], axis=1, keepdims=True)
    w_ref[...] = jnp.broadcast_to(local_sum, (1, 128))
    t_ref[me] = jnp.broadcast_to(local_sum, (1, 128))
    pl.semaphore_wait(barrier, DEVICES - 1)

    def send_forward(k, carry):
        to = shifted(at, (k * 37) % DEVICES)
        remote(x_ref.at[:, columns(flat(to))], slots_ref.at[me], sems["fwd_send"], sems["fwd_recv"], to, False)
        return carry

    def send_sum(k, carry):
        to = shifted(at, (k * 37) % DEVICES)
        remote(w_ref, t_ref.at[me], sems["sum_send"], sems["sum_recv"], to, False)
        return carry

    lax.fori_loop(1, DEVICES, send_forward, 0)
    lax.fori_loop(1, DEVICES, send_sum, 0)

    row = lax.broadcasted_iota(jnp.int32, (TILE, 128), 0)
    lane = lax.broadcasted_iota(jnp.int32, (TILE, 128), 1)
    place_mask[...] = jnp.where(row % SHARE == lane, 1.0, 0.0)
    owner_row = lax.broadcasted_iota(jnp.int32, (OWNERS, TILE), 0)
    owner_lane = lax.broadcasted_iota(jnp.int32, (OWNERS, TILE), 1)
    owner_mask[...] = jnp.where(owner_lane // SHARE == owner_row, 1.0, 0.0).astype(low)
    for g in range(4):
        stage[g, pl.ds(TILE, 8), :] = jnp.zeros((8, 128), f32)
    vec_ref[...] = jnp.zeros(vec_ref.shape, f32)
    vec_ref[pl.ds(0, 2), :] = bias_in[...]
    vec_ref[pl.ds(2, 1), :] = head_ref[...]
    for i in range(WIDTH // 128):
        col[pl.ds(i * 128, 128), :] = vec_ref[:, pl.ds(i * 128, 128)].T
    start[pl.ds(0, 128), :] = dense_ref[...]
    for load in loads:
        load.wait()
    for l in range(2):
        in_t[l] = in_ref[l].T
        out_t[l] = out_ref[l].T
    own.wait()
    most = slots_ref.at[pl.ds(0, DEVICES - 1)]
    pltpu.make_async_copy(most, most, sems["fwd_recv"]).wait()

    def gather(b, carry):
        cols_ref[pl.ds(pl.multiple_of(b * 16, 16), 16), :] = slots_ref[slot_ref[b]]
        return carry

    lax.fori_loop(0, BLOCKS, gather, 0, unroll=8)
    for n, (which, t, column, width) in enumerate(table_rows()):
        start[pl.ds(128 + n * 128, 128), :] = contract(
            projections[which][t], cols_ref[pl.ds(column, width), :], 0, 0).astype(low)

    hidden0 = contract(in_t[0], start[...], 1, 0).astype(low)

    def tile(i):
        return pl.ds(pl.multiple_of(i * TILE, 16), TILE)

    def forward0(i, carry):
        here = tile(i)
        gate = contract(out_t[0, here, :], hidden0, 1, 0) + col[here, 0:1]
        gate0[here, :] = gate
        s = start[here, :].astype(f32)
        layer[here, :] = (s * gate + s).astype(low)
        return carry

    lax.fori_loop(0, TILES, forward0, 0)
    hidden1 = contract(in_t[1], layer[...], 1, 0).astype(low)

    def forward1(i, logit):
        here = tile(i)
        gate = contract(out_t[1, here, :], hidden1, 1, 0) + col[here, 1:2]
        gate1[here, :] = gate
        last = (start[here, :].astype(f32) * gate + layer[here, :].astype(f32)).astype(low).astype(f32)
        return logit + jnp.sum((col[here, 2:3] * last).reshape(TILE // 8, 8, ROWS), axis=0)

    logit = lax.fori_loop(0, TILES, forward1, jnp.zeros((8, ROWS), f32))
    logit = jnp.sum(logit, axis=0, keepdims=True)
    signal = weight_ref[...] * (jax.nn.sigmoid(logit) - label_ref[...].astype(f32))

    def keep_bias(l, i, gate_grad):
        sums = jnp.sum(gate_grad, axis=1, keepdims=True)
        spread = (place_mask[...] * sums).astype(low)
        bias_ref[l, pl.ds(pl.multiple_of(i * OWNERS, 16), OWNERS), :] = contract(owner_mask[...], spread, 1, 0)

    def backward1(i, carry):
        here = tile(i)
        gate_grad = start[here, :].astype(f32) * (col[here, 2:3] * signal)
        keep_bias(1, i, gate_grad)
        low1[here, :] = gate_grad.astype(low)
        return carry

    lax.fori_loop(0, TILES, backward1, 0)
    grad1 = contract(out_ref[1], low1[...], 1, 0).astype(low)
    bias_row = lax.broadcasted_iota(jnp.int32, (SLOT, 128), 0) == SHARE
    reductions = [
        Reduction(l, at, grads[l], core_bufs[l], rs_bufs[l], sems, remote) for l in range(2)]

    def pack(l, i, in_term, out_term):
        for h in range(2):
            stage[h, pl.ds(0, TILE), :] = in_term[:, h * 128:(h + 1) * 128]
            stage[2 + h, pl.ds(0, TILE), :] = out_term[:, h * 128:(h + 1) * 128]
        for o in range(OWNERS):
            for g in range(4):
                piece = stage[g, pl.ds(SHARE * o, SLOT), :]
                if g == 0:
                    piece = jnp.where(bias_row, bias_ref[l, pl.ds(i * OWNERS + o, 1), :], piece)
                grads[l][i // 2, 2 * (i % 2) + o // 8, (o // 2) % 4, o % 2, pl.ds(g * SLOT, SLOT), :] = (
                    piece.astype(low))

        @pl.when(i > 0)
        def _():
            reductions[l].send_tile(i - 1)

    def backward0(i, carry):
        here = tile(i)
        pack(1, i, contract(layer[here, :], grad1, 1, 1), contract(low1[here, :], hidden1, 1, 1))
        above = col[here, 2:3] * signal
        upstream = above + contract(in_ref[1, here, :], grad1, 1, 0)
        gate_grad = start[here, :].astype(f32) * upstream
        keep_bias(0, i, gate_grad)
        low0[here, :] = gate_grad.astype(low)
        gate0[here, :] = gate1[here, :] * above + gate0[here, :] * upstream + upstream
        return carry

    lax.fori_loop(0, TILES, backward0, 0)
    reductions[1].send_tile(TILES - 1)
    grad0 = contract(out_ref[0], low0[...], 1, 0).astype(low)
    reductions[1].first()

    def finish(i, carry):
        here = tile(i)
        low1[here, :] = (gate0[here, :] + contract(in_ref[0, here, :], grad0, 1, 0)).astype(low)
        return carry

    lax.fori_loop(0, TILES, finish, 0)
    for n, (which, t, column, width) in enumerate(table_rows()):
        lg_ref[pl.ds(column // 16, width // 16)] = contract(
            projections[which][t], low1[pl.ds(128 + n * 128, 128), :], 1, 0).astype(low).reshape(
                width // 16, 16, ROWS)

    def spread(s, carry):
        sg_ref[s] = lg_ref[block_ref[s]]
        return carry

    lax.fori_loop(0, BLOCKS, spread, 0, unroll=8)
    reductions[1].middle()

    own_back = pltpu.make_async_copy(sg_ref.at[me], back_ref.at[:, columns(me)], sems["local"].at[5])
    own_back.start()

    def send_back(k, carry):
        to = shifted(at, (k * 37) % DEVICES)
        remote(sg_ref.at[flat(to)], back_ref.at[:, columns(me)], sems["back_send"], sems["back_recv"], to, False)
        return carry

    lax.fori_loop(1, 64, send_back, 0)

    def terms0(i, carry):
        here = tile(i)
        pack(0, i, contract(start[here, :], grad0, 1, 1), contract(low0[here, :], hidden0, 1, 1))
        return carry

    lax.fori_loop(0, TILES, terms0, 0)
    reductions[0].send_tile(TILES - 1)
    reductions[1].second()
    reductions[0].first()
    lax.fori_loop(64, 96, send_back, 0)
    reductions[1].third()
    reductions[0].middle()
    lax.fori_loop(96, DEVICES, send_back, 0)
    reductions[1].last(sums_ref)
    reductions[0].second()
    small = t_ref.at[pl.ds(0, DEVICES - 1)]
    pltpu.make_async_copy(small, small, sems["sum_recv"]).wait()
    total_ref[...] = jnp.sum(t_ref[...], axis=0)
    reductions[0].third()
    reductions[0].last(sums_ref)

    own_back.wait()
    for copy in sent:
        copy.wait_send()
    for reduction in reductions:
        reduction.wait_core("core_send")
    pltpu.make_async_copy(small, small, sems["sum_send"]).wait()
    pltpu.make_async_copy(most, most, sems["fwd_send"]).wait()
    pltpu.make_async_copy(most, most, sems["back_send"]).wait()
    pltpu.make_async_copy(most, most, sems["back_recv"]).wait()


def whole(slot_of_block, block_of_slot, pooled, dense, labels, weights, wide, mid, narrow, cross_in, cross_out, bias,
          head):
    vmem = pl.BlockSpec(memory_space=VM)
    smem = pl.BlockSpec(memory_space=pltpu.SMEM)
    hbm = pl.BlockSpec(memory_space=pl.ANY)
    low, f32 = jnp.bfloat16, jnp.float32
    activation = VM((WIDTH, ROWS), low)
    full = VM((WIDTH, ROWS), f32)
    scratch = [
        VM((DEVICES, 16, ROWS), low), VM((1, 128), f32), VM((DEVICES, 1, 128), f32),
        VM((2, WIDTH, 256), low), VM((2, 256, WIDTH), low), VM((2, 256, WIDTH), low), VM((2, WIDTH, 256), low),
        VM((8, WIDTH), f32), VM((WIDTH, 8), f32), VM((2048, ROWS), low), VM((DEVICES, 16, ROWS), low),
        VM((DEVICES, 16, ROWS), low),
        activation, activation, activation, activation, full, full,
        VM((4, TILE + 8, 128), f32), VM((2, DEVICES, 128), f32), VM((OWNERS, TILE), low), VM((TILE, 128), f32),
    ]
    scratch += [VM((4, 4, 4, 2, OWNED, 128), low)] * 2 + [VM((4, 4, 4, OWNED, 128), low)] * 2
    for l in range(2):
        for lo, hi, _ in PARTS[l]:
            n = hi - lo
            scratch += [VM((2, 4, n, 128), low), VM((2, 4, n, 128), low), VM((4, 4, n, 128), low),
                        VM((4, 4, n, 128), low), VM((3, 4, n, 128), low), VM((3, n, 128), low)]
    scratch += [pltpu.SemaphoreType.DMA(shape) if shape else pltpu.SemaphoreType.DMA for _, shape in SEMS]
    return pl.pallas_call(
        whole_kernel,
        out_shape=(jax.ShapeDtypeStruct((2, OWNED, 128), f32),
                   jax.ShapeDtypeStruct((16, DEVICES * ROWS), low),
                   jax.ShapeDtypeStruct((1, 128), f32)),
        in_specs=[smem, smem, hbm] + [vmem] * 6 + [hbm, hbm, vmem, vmem],
        out_specs=(vmem, vmem, vmem),
        scratch_shapes=scratch,
        compiler_params=pltpu.CompilerParams(
            has_side_effects=True, collective_id=0, vmem_limit_bytes=60 * 1024 * 1024),
        name="whole",
    )(slot_of_block, block_of_slot, pooled, dense, labels, weights, wide, mid, narrow, cross_in, cross_out, bias, head)


def body(
    pooled,
    slot_of_block,
    dense_part,
    labels,
    sample_weight,
    proj_wide,
    proj_mid,
    proj_narrow,
    cross_in,
    cross_out,
    cross_bias,
    head_weight,
):
    batch_rows = pooled.shape[2]
    numbers = jnp.arange(BLOCKS, dtype=jnp.int32)
    block_of_slot = jnp.sum(jnp.where(slot_of_block[None, :] == numbers[:, None], numbers[None, :], 0), 1)
    sums, returned, total = whole(
        slot_of_block,
        block_of_slot,
        pooled.reshape(BLOCK_WIDTH, batch_rows),
        dense_part,
        labels[None],
        sample_weight[None],
        proj_wide,
        proj_mid,
        proj_narrow,
        cross_in,
        cross_out,
        cross_bias,
        head_weight[None],
    )
    scale = batch_rows / total[0, 0]
    sums = sums.reshape(2, 2, 2, SLOT, 128) * scale
    whole_sums = jnp.moveaxis(sums[:, :, :, :SHARE], 2, 3).reshape(2, 2, SHARE, 256)
    grad_bias = sums[:, 0, 0, SHARE, :SHARE]
    pooled_grad = (returned.astype(jnp.float32) * scale).reshape(BLOCK_WIDTH, 1, batch_rows)
    return (pooled_grad, whole_sums[:, 0], jnp.swapaxes(whole_sums[:, 1], 1, 2), grad_bias)


def solution(mesh):
    finer = Mesh(mesh.devices.reshape(4, 4, 4, mesh.shape["rep"]), ("dp_0", "dp_1", "dp_2", "rep"))
    return jax.shard_map(
        body,
        mesh=finer,
        in_specs=(
            P(None, DP_REP, None),
            P(),
            P(None, DP_REP),
            P(DP_REP),
            P(DP_REP),
            P(),
            P(),
            P(),
            P(),
            P(),
            P(),
            P(),
        ),
        out_specs=(
            P(None, DP_REP, None),
            P(None, DP_REP, None),
            P(None, None, DP_REP),
            P(None, DP_REP),
        ),
        check_vma=False,
    )
```

```python
import jax
import jax.numpy as jnp
from jax import lax
from jax.experimental import pallas as pl
from jax.experimental.pallas import tpu as pltpu
from jax.sharding import Mesh
from jax.sharding import PartitionSpec as P

BLOCK_WIDTH = 16
BLOCKS = 128
BATCH_ROWS = 32768
DP_REP = ("dp_0", "dp_1", "dp_2", "rep")
AXES = DP_REP
MESH = pl.DeviceIdType.MESH
DEVICES = 128
ROWS = 256
TILE = 432
TILES = 8
OWNERS = 16
WIDTH = 3456
SHARE = 27
SLOT = 32
OWNED = 128
VM = pltpu.VMEM
PARTS = (
    ((0, 32, (0, 1, 2)), (32, 80, (1, 2, 0)), (80, 128, (2, 0, 1))),
    ((0, 48, (0, 1, 2)), (48, 96, (1, 2, 0)), (96, 128, (2, 0, 1))),
)
TURN_X = (0, 1, 2, 3, 1, 2, 3, 0)
TURN_Z = (0, 2, 1, 3, 3, 1, 0, 2)
HALVES = (pl.ds(0, 2), pl.ds(2, 2))


def place():
    return tuple(lax.axis_index(a) for a in AXES)


def flat(at):
    return ((at[0] * 4 + at[1]) * 4 + at[2]) * 2 + at[3]


def columns(device):
    return pl.ds(pl.multiple_of(device * ROWS, ROWS), ROWS)


def contract(a, b, da, db):
    return lax.dot_general(a, b, (((da,), (db,)), ((), ())), preferred_element_type=jnp.float32)


def table_rows():
    rows = []
    column = 0
    for which, (count, width) in enumerate(((6, 256), (4, 64), (16, 16))):
        for t in range(count):
            rows.append((which, t, column, width))
            column += width
    return rows


def sub(ref, chosen, tail):
    return ref.at[tuple(chosen.get(d, slice(None)) for d in range(3)) + tail]


class Reduction:
    def __init__(self, layer, at, grads, core_buf, bufs, sems, remote):
        self.layer, self.at, self.core = layer, at, at[3]
        self.grads, self.core_buf, self.bufs, self.sems = grads, core_buf, bufs, sems
        self.remote = remote
        self.one, self.two, self.three, self.kept = {}, {}, {}, {}

    def moved(self, d, k):
        return tuple((a + k) % 4 if i == d else a for i, a in enumerate(self.at[:3])) + (self.core,)

    def send_tile(self, i):
        there = pl.ds(2 * (i % 2), 2)
        self.remote(
            self.grads.at[i // 2, there, :, 1 - self.core], self.core_buf.at[i // 2, there],
            self.sems["core_send"].at[self.layer], self.sems["core_recv"].at[self.layer],
            self.at[:3] + (1 - self.core,), False)

    def wait_core(self, which):
        pltpu.make_async_copy(self.core_buf, self.core_buf, self.sems[which].at[self.layer]).wait()

    def step(self, which, p, n, src, dst, d, k):
        return self.remote(src, dst, self.sems[which + "_send"].at[self.layer, p, n],
                           self.sems[which + "_recv"].at[self.layer, p, n], self.moved(d, k), True)

    def first(self):
        self.wait_core("core_recv")

        def fold(b, carry):
            x, z = b // 4, b % 4
            for y in range(4):
                self.core_buf[x, z, y] = self.core_buf[x, z, y] + self.grads[x, z, y, self.core]
            return carry

        lax.fori_loop(0, 16, fold, 0)
        for p, (lo, hi, (d, _, _)) in enumerate(PARTS[self.layer]):
            tail = (pl.ds(lo, hi - lo), slice(None))
            for k in range(4):
                self.kept[p, k] = sub(self.core_buf, {d: (self.at[d] + k) % 4}, tail)
            ra, rb = self.bufs[p][:2]
            self.one[p, 0] = self.step("one", p, 0, self.kept[p, 2].at[HALVES[0]], ra, d, 1)
            self.one[p, 1] = self.step("one", p, 1, self.kept[p, 2].at[HALVES[1]], rb, d, 3)
        for p, (lo, hi, (d, _, _)) in enumerate(PARTS[self.layer]):
            rp, rm = self.bufs[p][2:4]
            self.one[p, 2] = self.step(
                "one", p, 2, self.kept[p, 1].at[HALVES[1]], rp.at[HALVES[1]], d, 1)
            self.one[p, 3] = self.step(
                "one", p, 3, self.kept[p, 3].at[HALVES[0]], rm.at[HALVES[0]], d, 3)

    def middle(self):
        for p, (lo, hi, (d, _, _)) in enumerate(PARTS[self.layer]):
            ra, rb, rp, rm = self.bufs[p][:4]
            self.one[p, 0].wait_recv()
            up = self.kept[p, 1].at[HALVES[0]]
            up[...] = up[...] + ra[...]
            self.one[p, 4] = self.step("one", p, 4, up, rp.at[HALVES[0]], d, 1)
            self.one[p, 1].wait_recv()
            down = self.kept[p, 3].at[HALVES[1]]
            down[...] = down[...] + rb[...]
            self.one[p, 5] = self.step("one", p, 5, down, rm.at[HALVES[1]], d, 3)

    def second(self):
        f32 = jnp.float32
        for p, (lo, hi, (d, e, f)) in enumerate(PARTS[self.layer]):
            rp, rm, r2 = self.bufs[p][2:5]
            for n in range(2, 6):
                self.one[p, n].wait_recv()
            total = self.kept[p, 0]
            for i in range(4):
                total[i] = (total[i].astype(f32) + rp[i].astype(f32) + rm[i].astype(f32)).astype(jnp.bfloat16)
            for k in (2, 1, 3):
                self.two[p, k] = self.step(
                    "two", p, k - 1, self.pick(p, {e: (self.at[e] + k) % 4}), r2.at[k - 1], e, k)

    def pick(self, p, chosen):
        d = PARTS[self.layer][p][2][0]
        return self.kept[p, 0].at[tuple(chosen.get(i, slice(None)) for i in range(3) if i != d)]

    def third(self):
        f32 = jnp.float32
        self.held = {}
        for p, (lo, hi, (d, e, f)) in enumerate(PARTS[self.layer]):
            r2, r3 = self.bufs[p][4:6]
            for k in (1, 2, 3):
                self.two[p, k].wait_recv()
            mine = self.pick(p, {e: self.at[e]})
            mine[...] = (mine[...].astype(f32) + r2[0].astype(f32) + r2[1].astype(f32)
                         + r2[2].astype(f32)).astype(jnp.bfloat16)
            self.held[p] = mine
            for k in (2, 1, 3):
                self.three[p, k] = self.step(
                    "three", p, k - 1, mine.at[(self.at[f] + k) % 4], r3.at[k - 1], f, k)

    def last(self, out_ref):
        f32 = jnp.float32
        for p, (lo, hi, (d, e, f)) in enumerate(PARTS[self.layer]):
            r3 = self.bufs[p][5]
            for k in (1, 2, 3):
                self.three[p, k].wait_recv()
            out_ref[self.layer, pl.ds(lo, hi - lo), :] = (
                self.held[p].at[self.at[f]][...].astype(f32) + r3[0].astype(f32) + r3[1].astype(f32)
                + r3[2].astype(f32))


SEMS = (("core_send", (2,)), ("core_recv", (2,)), ("one_send", (2, 3, 6)), ("one_recv", (2, 3, 6)),
        ("two_send", (2, 3, 3)), ("two_recv", (2, 3, 3)), ("three_send", (2, 3, 3)), ("three_recv", (2, 3, 3)),
        ("fwd_send", ()), ("fwd_recv", ()), ("sum_send", ()), ("sum_recv", ()), ("back_send", ()),
        ("back_recv", ()), ("local", (7,)))


def whole_kernel(slot_ref, block_ref, x_ref, dense_ref, label_ref, weight_ref, wide_ref, mid_ref, narrow_ref,
                 in_hbm, out_hbm, bias_in, head_ref, sums_ref, back_ref, total_ref,
                 slots_ref, w_ref, t_ref, in_ref, out_ref, in_t, out_t, vec_ref, col, cols_ref, sg_ref, lg_ref, start, layer,
                 low0, low1, gate0, gate1, stage, bias_ref, owner_mask, place_mask, *rest):
    low = jnp.bfloat16
    f32 = jnp.float32
    projections = (wide_ref, mid_ref, narrow_ref)
    grads, core_bufs, rest = rest[:2], rest[2:4], rest[4:]
    rs_bufs = [[rest[(l * 3 + p) * 6:(l * 3 + p + 1) * 6] for p in range(3)] for l in range(2)]
    sems = {name: sem for (name, _), sem in zip(SEMS, rest[36:-1])}
    sems["round"] = rest[-1]
    at = place()
    me = flat(at)
    sent = []

    def remote(src, dst, ss, rs, to, keep):
        copy = pltpu.make_async_remote_copy(
            src_ref=src, dst_ref=dst, send_sem=ss, recv_sem=rs, device_id=to, device_id_type=MESH)
        copy.start()
        if keep:
            sent.append(copy)
        return copy

    barrier = pltpu.get_barrier_semaphore()

    lines = [[tuple((a + k) % 4 if i == d else a for i, a in enumerate(at[:3])) + at[3:] for k in (1, 2, 3)]
             for d in range(3)]
    near = [at[:3] + (1 - at[3],)] + lines[0] + lines[1] + lines[2]
    for device in near:
        pl.semaphore_signal(barrier, inc=1, device_id=device, device_id_type=MESH)
    loads = []
    for l in range(2):
        loads.append(pltpu.make_async_copy(in_hbm.at[l], in_ref.at[l], sems["local"].at[l]))
        loads.append(pltpu.make_async_copy(out_hbm.at[l], out_ref.at[l], sems["local"].at[2 + l]))
    for load in loads:
        load.start()
    own = pltpu.make_async_copy(x_ref.at[:, columns(me)], slots_ref.at[me], sems["local"].at[4])
    own.start()
    local_sum = jnp.sum(weight_ref[...], axis=1, keepdims=True)
    w_ref[...] = jnp.broadcast_to(local_sum, (1, 128))
    t_ref[me] = jnp.broadcast_to(local_sum, (1, 128))
    pl.semaphore_wait(barrier, len(near))
    for d in (2, 1, 0):
        for device in lines[d]:
            pl.semaphore_signal(sems["round"].at[d], inc=1, device_id=device, device_id_type=MESH)
        pl.semaphore_wait(sems["round"].at[d], 3)

    def to_all(lo, hi, send):
        def some(i, carry):
            xs = [(at[0] + i + q) % 4 for q in range(4)]
            zs = [(at[1] + i // 4 + q) % 4 for q in range(4)]
            for n in range(8):
                to = (xs[TURN_X[n]], zs[TURN_Z[n]], ys[n // 2], cores[n % 2])
                if n == 0:
                    @pl.when(i > 0)
                    def _():
                        send(to)
                else:
                    send(to)
            return carry

        ys = [(at[2] + q) % 4 for q in range(4)]
        cores = [at[3], 1 - at[3]]
        lax.fori_loop(lo, hi, some, 0)

    def send_forward(to):
        remote(x_ref.at[:, columns(flat(to))], slots_ref.at[me], sems["fwd_send"], sems["fwd_recv"], to, False)

    def send_sum(to):
        remote(w_ref, t_ref.at[me], sems["sum_send"], sems["sum_recv"], to, False)

    def send_back(to):
        remote(sg_ref.at[flat(to)], back_ref.at[:, columns(me)], sems["back_send"], sems["back_recv"], to, False)

    to_all(0, 16, send_forward)

    row = lax.broadcasted_iota(jnp.int32, (TILE, 128), 0)
    lane = lax.broadcasted_iota(jnp.int32, (TILE, 128), 1)
    place_mask[...] = jnp.where(row % SHARE == lane, 1.0, 0.0)
    owner_row = lax.broadcasted_iota(jnp.int32, (OWNERS, TILE), 0)
    owner_lane = lax.broadcasted_iota(jnp.int32, (OWNERS, TILE), 1)
    owner_mask[...] = jnp.where(owner_lane // SHARE == owner_row, 1.0, 0.0).astype(low)
    for g in range(4):
        stage[g, pl.ds(TILE, 8), :] = jnp.zeros((8, 128), f32)
    vec_ref[...] = jnp.zeros(vec_ref.shape, f32)
    vec_ref[pl.ds(0, 2), :] = bias_in[...]
    for i in range(WIDTH // 128):
        vec_ref[2, pl.ds(i * 128, 128)] = head_ref[pl.ds(i * 128, 128)]
    for i in range(WIDTH // 128):
        col[pl.ds(i * 128, 128), :] = vec_ref[:, pl.ds(i * 128, 128)].T
    start[pl.ds(0, 128), :] = dense_ref[...]
    for load in loads:
        load.wait()
    for l in range(2):
        in_t[l] = in_ref[l].T
        out_t[l] = out_ref[l].T
    to_all(0, 16, send_sum)
    own.wait()
    most = slots_ref.at[pl.ds(0, DEVICES - 1)]
    pltpu.make_async_copy(most, most, sems["fwd_recv"]).wait()

    def gather(b, carry):
        cols_ref[pl.ds(pl.multiple_of(b * 16, 16), 16), :] = slots_ref[slot_ref[b]]
        return carry

    lax.fori_loop(0, BLOCKS, gather, 0, unroll=8)
    for n, (which, t, column, width) in enumerate(table_rows()):
        start[pl.ds(128 + n * 128, 128), :] = contract(
            projections[which][t], cols_ref[pl.ds(column, width), :], 0, 0).astype(low)

    hidden0 = contract(in_t[0], start[...], 1, 0).astype(low)

    def tile(i):
        return pl.ds(pl.multiple_of(i * TILE, 16), TILE)

    def forward0(i, carry):
        here = tile(i)
        gate = contract(out_t[0, here, :], hidden0, 1, 0) + col[here, 0:1]
        gate0[here, :] = gate
        s = start[here, :].astype(f32)
        layer[here, :] = (s * gate + s).astype(low)
        return carry

    lax.fori_loop(0, TILES, forward0, 0)
    hidden1 = contract(in_t[1], layer[...], 1, 0).astype(low)

    def forward1(i, logit):
        here = tile(i)
        gate = contract(out_t[1, here, :], hidden1, 1, 0) + col[here, 1:2]
        gate1[here, :] = gate
        last = (start[here, :].astype(f32) * gate + layer[here, :].astype(f32)).astype(low).astype(f32)
        return logit + jnp.sum((col[here, 2:3] * last).reshape(TILE // 8, 8, ROWS), axis=0)

    logit = lax.fori_loop(0, TILES, forward1, jnp.zeros((8, ROWS), f32))
    logit = jnp.sum(logit, axis=0, keepdims=True)
    signal = weight_ref[...] * (jax.nn.sigmoid(logit) - label_ref[...].astype(f32))

    def keep_bias(l, i, gate_grad):
        sums = jnp.sum(gate_grad, axis=1, keepdims=True)
        spread = (place_mask[...] * sums).astype(low)
        bias_ref[l, pl.ds(pl.multiple_of(i * OWNERS, 16), OWNERS), :] = contract(owner_mask[...], spread, 1, 0)

    def backward1(i, carry):
        here = tile(i)
        gate_grad = start[here, :].astype(f32) * (col[here, 2:3] * signal)
        keep_bias(1, i, gate_grad)
        low1[here, :] = gate_grad.astype(low)
        return carry

    lax.fori_loop(0, TILES, backward1, 0)
    grad1 = contract(out_ref[1], low1[...], 1, 0).astype(low)
    bias_row = lax.broadcasted_iota(jnp.int32, (SLOT, 128), 0) == SHARE
    reductions = [
        Reduction(l, at, grads[l], core_bufs[l], rs_bufs[l], sems, remote) for l in range(2)]

    def pack(l, i, in_term, out_term):
        for h in range(2):
            stage[h, pl.ds(0, TILE), :] = in_term[:, h * 128:(h + 1) * 128]
            stage[2 + h, pl.ds(0, TILE), :] = out_term[:, h * 128:(h + 1) * 128]
        for o in range(OWNERS):
            for g in range(4):
                piece = stage[g, pl.ds(SHARE * o, SLOT), :]
                if g == 0:
                    piece = jnp.where(bias_row, bias_ref[l, pl.ds(i * OWNERS + o, 1), :], piece)
                grads[l][i // 2, 2 * (i % 2) + o // 8, (o // 2) % 4, o % 2, pl.ds(g * SLOT, SLOT), :] = (
                    piece.astype(low))

        @pl.when(i > 0)
        def _():
            reductions[l].send_tile(i - 1)

    def backward0(i, carry):
        here = tile(i)
        pack(1, i, contract(layer[here, :], grad1, 1, 1), contract(low1[here, :], hidden1, 1, 1))
        above = col[here, 2:3] * signal
        upstream = above + contract(in_ref[1, here, :], grad1, 1, 0)
        gate_grad = start[here, :].astype(f32) * upstream
        keep_bias(0, i, gate_grad)
        low0[here, :] = gate_grad.astype(low)
        gate0[here, :] = gate1[here, :] * above + gate0[here, :] * upstream + upstream
        return carry

    lax.fori_loop(0, TILES, backward0, 0)
    reductions[1].send_tile(TILES - 1)
    grad0 = contract(out_ref[0], low0[...], 1, 0).astype(low)
    reductions[1].first()

    def finish(i, carry):
        here = tile(i)
        low1[here, :] = (gate0[here, :] + contract(in_ref[0, here, :], grad0, 1, 0)).astype(low)
        return carry

    lax.fori_loop(0, TILES, finish, 0)
    for n, (which, t, column, width) in enumerate(table_rows()):
        lg_ref[pl.ds(column // 16, width // 16)] = contract(
            projections[which][t], low1[pl.ds(128 + n * 128, 128), :], 1, 0).astype(low).reshape(
                width // 16, 16, ROWS)

    def spread(s, carry):
        sg_ref[s] = lg_ref[block_ref[s]]
        return carry

    lax.fori_loop(0, BLOCKS, spread, 0, unroll=8)

    own_back = pltpu.make_async_copy(sg_ref.at[me], back_ref.at[:, columns(me)], sems["local"].at[5])
    own_back.start()
    to_all(0, 5, send_back)

    def terms0(i, carry):
        here = tile(i)
        pack(0, i, contract(start[here, :], grad0, 1, 1), contract(low0[here, :], hidden0, 1, 1))
        return carry

    lax.fori_loop(0, TILES, terms0, 0)
    reductions[0].send_tile(TILES - 1)
    reductions[1].middle()
    to_all(5, 7, send_back)
    reductions[0].first()
    reductions[1].second()
    to_all(7, 10, send_back)
    reductions[0].middle()
    reductions[1].third()
    to_all(10, 13, send_back)
    reductions[0].second()
    reductions[1].last(sums_ref)
    to_all(13, 16, send_back)
    small = t_ref.at[pl.ds(0, DEVICES - 1)]
    pltpu.make_async_copy(small, small, sems["sum_recv"]).wait()
    total_ref[...] = jnp.sum(t_ref[...], axis=0)
    reductions[0].third()
    reductions[0].last(sums_ref)

    own_back.wait()
    for copy in sent:
        copy.wait_send()
    for reduction in reductions:
        reduction.wait_core("core_send")
    pltpu.make_async_copy(small, small, sems["sum_send"]).wait()
    pltpu.make_async_copy(most, most, sems["fwd_send"]).wait()
    pltpu.make_async_copy(most, most, sems["back_send"]).wait()
    pltpu.make_async_copy(most, most, sems["back_recv"]).wait()


def whole(slot_of_block, block_of_slot, pooled, dense, labels, weights, wide, mid, narrow, cross_in, cross_out, bias,
          head):
    vmem = pl.BlockSpec(memory_space=VM)
    smem = pl.BlockSpec(memory_space=pltpu.SMEM)
    hbm = pl.BlockSpec(memory_space=pl.ANY)
    low, f32 = jnp.bfloat16, jnp.float32
    activation = VM((WIDTH, ROWS), low)
    full = VM((WIDTH, ROWS), f32)
    scratch = [
        VM((DEVICES, 16, ROWS), low), VM((1, 128), f32), VM((DEVICES, 1, 128), f32),
        VM((2, WIDTH, 256), low), VM((2, 256, WIDTH), low), VM((2, 256, WIDTH), low), VM((2, WIDTH, 256), low),
        VM((8, WIDTH), f32), VM((WIDTH, 8), f32), VM((2048, ROWS), low), VM((DEVICES, 16, ROWS), low),
        VM((DEVICES, 16, ROWS), low),
        activation, activation, activation, activation, full, full,
        VM((4, TILE + 8, 128), f32), VM((2, DEVICES, 128), f32), VM((OWNERS, TILE), low), VM((TILE, 128), f32),
    ]
    scratch += [VM((4, 4, 4, 2, OWNED, 128), low)] * 2 + [VM((4, 4, 4, OWNED, 128), low)] * 2
    for l in range(2):
        for lo, hi, _ in PARTS[l]:
            n = hi - lo
            scratch += [VM((2, 4, n, 128), low), VM((2, 4, n, 128), low), VM((4, 4, n, 128), low),
                        VM((4, 4, n, 128), low), VM((3, 4, n, 128), low), VM((3, n, 128), low)]
    scratch += [pltpu.SemaphoreType.DMA(shape) if shape else pltpu.SemaphoreType.DMA for _, shape in SEMS]
    scratch.append(pltpu.SemaphoreType.REGULAR((3,)))
    return pl.pallas_call(
        whole_kernel,
        out_shape=(jax.ShapeDtypeStruct((2, OWNED, 128), f32),
                   jax.ShapeDtypeStruct((16, DEVICES * ROWS), low),
                   jax.ShapeDtypeStruct((1, 128), f32)),
        in_specs=[smem, smem, hbm] + [vmem] * 6 + [hbm, hbm, vmem, vmem],
        out_specs=(vmem, vmem, vmem),
        scratch_shapes=scratch,
        compiler_params=pltpu.CompilerParams(
            has_side_effects=True, collective_id=0, vmem_limit_bytes=60 * 1024 * 1024),
        name="whole",
    )(slot_of_block, block_of_slot, pooled, dense, labels, weights, wide, mid, narrow, cross_in, cross_out, bias, head)


PIECES = 4


def post_kernel(back_ref, sums_ref, total_ref, pooled_ref, in_ref, out_ref, bias_ref):
    scale = BATCH_ROWS / total_ref[...]
    many = back_ref.shape[1] // 128
    flat_rows = pooled_ref.reshape(BLOCK_WIDTH * many, 128)

    def move(j, carry):
        at = pl.ds(pl.multiple_of(j * 128, 128), 128)
        flat_rows[pl.ds(j, BLOCK_WIDTH, stride=many), :] = back_ref[:, at].astype(jnp.float32) * scale
        return carry

    lax.fori_loop(0, many, move, 0, unroll=8)

    @pl.when(pl.program_id(0) == 0)
    def _():
        for l in range(2):
            for h in range(2):
                rows = pl.ds(2 * h + l, SHARE, stride=4)
                in_ref[rows, :] = sums_ref[l, pl.ds(h * SLOT, SHARE), :] * scale
                out_ref[rows, :] = sums_ref[l, pl.ds((2 + h) * SLOT, SHARE), :] * scale
            bias_ref[pl.ds(l, 1), :] = (sums_ref[l, pl.ds(SHARE, 1), :] * scale)[:, :SHARE]


def post(returned, sums, total):
    f32 = jnp.float32
    many = DEVICES * ROWS // 128
    once = lambda shape: pl.BlockSpec(shape, lambda i: (0,) * len(shape))
    return pl.pallas_call(
        post_kernel,
        grid=(PIECES,),
        out_shape=(jax.ShapeDtypeStruct((BLOCK_WIDTH, many, 128), f32),
                   jax.ShapeDtypeStruct((4 * SHARE, 128), f32),
                   jax.ShapeDtypeStruct((4 * SHARE, 128), f32),
                   jax.ShapeDtypeStruct((2, SHARE), f32)),
        in_specs=[pl.BlockSpec((BLOCK_WIDTH, DEVICES * ROWS // PIECES), lambda i: (0, i)),
                  once((2, OWNED, 128)), once((1, 128))],
        out_specs=(pl.BlockSpec((BLOCK_WIDTH, many // PIECES, 128), lambda i: (0, i, 0)),
                   once((4 * SHARE, 128)), once((4 * SHARE, 128)), once((2, SHARE))),
        name="post",
    )(returned, sums, total)


def unpacked(rows):
    return jnp.transpose(rows.reshape(SHARE, 2, 2, 128), (2, 0, 1, 3)).reshape(2, SHARE, 256)


def body(
    pooled,
    slot_of_block,
    dense_part,
    labels,
    sample_weight,
    proj_wide,
    proj_mid,
    proj_narrow,
    cross_in,
    cross_out,
    cross_bias,
    head_weight,
):
    numbers = jnp.arange(BLOCKS, dtype=jnp.int32)
    block_of_slot = jnp.max(jnp.where(slot_of_block[None, :] == numbers[:, None], numbers[None, :], 0), 1)
    sums, returned, total = whole(
        slot_of_block,
        block_of_slot,
        pooled.reshape(BLOCK_WIDTH, BATCH_ROWS),
        dense_part,
        labels[None],
        sample_weight[None],
        proj_wide,
        proj_mid,
        proj_narrow,
        cross_in,
        cross_out,
        cross_bias,
        head_weight,
    )
    pooled_grad, grad_in, grad_out, grad_bias = post(returned, sums, total)
    return (
        pooled_grad.reshape(BLOCK_WIDTH, 1, BATCH_ROWS),
        unpacked(grad_in),
        jnp.swapaxes(unpacked(grad_out), 1, 2),
        grad_bias,
    )


def solution(mesh):
    finer = Mesh(mesh.devices.reshape(4, 4, 4, mesh.shape["rep"]), ("dp_0", "dp_1", "dp_2", "rep"))
    return jax.shard_map(
        body,
        mesh=finer,
        in_specs=(
            P(None, DP_REP, None),
            P(),
            P(None, DP_REP),
            P(DP_REP),
            P(DP_REP),
            P(),
            P(),
            P(),
            P(),
            P(),
            P(),
            P(),
        ),
        out_specs=(
            P(None, DP_REP, None),
            P(None, DP_REP, None),
            P(None, None, DP_REP),
            P(None, DP_REP),
        ),
        check_vma=False,
    )
```

```python
import jax
import jax.numpy as jnp
from jax import lax
from jax.experimental import pallas as pl
from jax.experimental.pallas import tpu as pltpu
from jax.sharding import Mesh
from jax.sharding import PartitionSpec as P

BLOCK_WIDTH = 16
BLOCKS = 128
BATCH_ROWS = 32768
DP_REP = ("dp_0", "dp_1", "dp_2", "rep")
AXES = DP_REP
MESH = pl.DeviceIdType.MESH
DEVICES = 128
ROWS = 256
TILE = 432
TILES = 8
OWNERS = 16
WIDTH = 3456
SHARE = 27
SLOT = 32
OWNED = 128
VM = pltpu.VMEM
PARTS = (
    ((0, 32, (0, 1, 2)), (32, 80, (1, 2, 0)), (80, 128, (2, 0, 1))),
    ((0, 48, (0, 1, 2)), (48, 96, (1, 2, 0)), (96, 128, (2, 0, 1))),
)


def known_after(x, z, y, c):
    others = (x != 0) + (c != 0)
    if others + (z != 0) + (y != 0) == 1:
        return 0
    if not z:
        return 1 if y and others == 1 else 3
    return 2 if others < 2 else 3


def sends_of(rounds):
    steps = [((k // 32), (k // 8) % 4, (k // 2) % 4, k % 2) for k in [(37 * i) % 128 for i in range(1, 128)]]
    steps = [step for step in steps if (known_after(*step) if sum(map(bool, step)) != 2 or not (
        step[1] and step[2]) else 1) == rounds]
    return sorted(steps, key=lambda step: -sum(min(v, 4 - v) for v in step[:3]))


FORWARD = [sends_of(rounds) for rounds in range(4)]
TURN_X = (0, 1, 2, 3, 1, 2, 3, 0)
TURN_Z = (0, 2, 1, 3, 3, 1, 0, 2)
HALVES = (pl.ds(0, 2), pl.ds(2, 2))


def place():
    return tuple(lax.axis_index(a) for a in AXES)


def flat(at):
    return ((at[0] * 4 + at[1]) * 4 + at[2]) * 2 + at[3]


def columns(device):
    return pl.ds(pl.multiple_of(device * ROWS, ROWS), ROWS)


def contract(a, b, da, db):
    return lax.dot_general(a, b, (((da,), (db,)), ((), ())), preferred_element_type=jnp.float32)


def table_rows():
    rows = []
    column = 0
    for which, (count, width) in enumerate(((6, 256), (4, 64), (16, 16))):
        for t in range(count):
            rows.append((which, t, column, width))
            column += width
    return rows


def sub(ref, chosen, tail):
    return ref.at[tuple(chosen.get(d, slice(None)) for d in range(3)) + tail]


class Reduction:
    def __init__(self, layer, at, grads, core_buf, bufs, sems, remote):
        self.layer, self.at, self.core = layer, at, at[3]
        self.grads, self.core_buf, self.bufs, self.sems = grads, core_buf, bufs, sems
        self.remote = remote
        self.one, self.two, self.three, self.kept = {}, {}, {}, {}

    def moved(self, d, k):
        return tuple((a + k) % 4 if i == d else a for i, a in enumerate(self.at[:3])) + (self.core,)

    def send_tile(self, i):
        there = pl.ds(2 * (i % 2), 2)
        self.remote(
            self.grads.at[i // 2, there, :, 1 - self.core], self.core_buf.at[i // 2, there],
            self.sems["core_send"].at[self.layer], self.sems["core_recv"].at[self.layer],
            self.at[:3] + (1 - self.core,), False)

    def wait_core(self, which):
        pltpu.make_async_copy(self.core_buf, self.core_buf, self.sems[which].at[self.layer]).wait()

    def step(self, which, p, n, src, dst, d, k):
        return self.remote(src, dst, self.sems[which + "_send"].at[self.layer, p, n],
                           self.sems[which + "_recv"].at[self.layer, p, n], self.moved(d, k), True)

    def first(self):
        self.wait_core("core_recv")

        def fold(b, carry):
            x, z = b // 4, b % 4
            for y in range(4):
                self.core_buf[x, z, y] = self.core_buf[x, z, y] + self.grads[x, z, y, self.core]
            return carry

        lax.fori_loop(0, 16, fold, 0)
        for p, (lo, hi, (d, _, _)) in enumerate(PARTS[self.layer]):
            tail = (pl.ds(lo, hi - lo), slice(None))
            for k in range(4):
                self.kept[p, k] = sub(self.core_buf, {d: (self.at[d] + k) % 4}, tail)
            ra, rb = self.bufs[p][:2]
            self.one[p, 0] = self.step("one", p, 0, self.kept[p, 2].at[HALVES[0]], ra, d, 1)
            self.one[p, 1] = self.step("one", p, 1, self.kept[p, 2].at[HALVES[1]], rb, d, 3)
        for p, (lo, hi, (d, _, _)) in enumerate(PARTS[self.layer]):
            rp, rm = self.bufs[p][2:4]
            self.one[p, 2] = self.step(
                "one", p, 2, self.kept[p, 1].at[HALVES[1]], rp.at[HALVES[1]], d, 1)
            self.one[p, 3] = self.step(
                "one", p, 3, self.kept[p, 3].at[HALVES[0]], rm.at[HALVES[0]], d, 3)

    def middle(self):
        for p, (lo, hi, (d, _, _)) in enumerate(PARTS[self.layer]):
            ra, rb, rp, rm = self.bufs[p][:4]
            self.one[p, 0].wait_recv()
            up = self.kept[p, 1].at[HALVES[0]]
            up[...] = up[...] + ra[...]
            self.one[p, 4] = self.step("one", p, 4, up, rp.at[HALVES[0]], d, 1)
            self.one[p, 1].wait_recv()
            down = self.kept[p, 3].at[HALVES[1]]
            down[...] = down[...] + rb[...]
            self.one[p, 5] = self.step("one", p, 5, down, rm.at[HALVES[1]], d, 3)

    def second(self):
        f32 = jnp.float32
        for p, (lo, hi, (d, e, f)) in enumerate(PARTS[self.layer]):
            rp, rm, r2 = self.bufs[p][2:5]
            for n in range(2, 6):
                self.one[p, n].wait_recv()
            total = self.kept[p, 0]
            for i in range(4):
                total[i] = (total[i].astype(f32) + rp[i].astype(f32) + rm[i].astype(f32)).astype(jnp.bfloat16)
            for k in (2, 1, 3):
                self.two[p, k] = self.step(
                    "two", p, k - 1, self.pick(p, {e: (self.at[e] + k) % 4}), r2.at[k - 1], e, k)

    def pick(self, p, chosen):
        d = PARTS[self.layer][p][2][0]
        return self.kept[p, 0].at[tuple(chosen.get(i, slice(None)) for i in range(3) if i != d)]

    def third(self):
        f32 = jnp.float32
        self.held = {}
        for p, (lo, hi, (d, e, f)) in enumerate(PARTS[self.layer]):
            r2, r3 = self.bufs[p][4:6]
            for k in (1, 2, 3):
                self.two[p, k].wait_recv()
            mine = self.pick(p, {e: self.at[e]})
            mine[...] = (mine[...].astype(f32) + r2[0].astype(f32) + r2[1].astype(f32)
                         + r2[2].astype(f32)).astype(jnp.bfloat16)
            self.held[p] = mine
            for k in (2, 1, 3):
                self.three[p, k] = self.step(
                    "three", p, k - 1, mine.at[(self.at[f] + k) % 4], r3.at[k - 1], f, k)

    def last(self, out_ref):
        f32 = jnp.float32
        for p, (lo, hi, (d, e, f)) in enumerate(PARTS[self.layer]):
            r3 = self.bufs[p][5]
            for k in (1, 2, 3):
                self.three[p, k].wait_recv()
            out_ref[self.layer, pl.ds(lo, hi - lo), :] = (
                self.held[p].at[self.at[f]][...].astype(f32) + r3[0].astype(f32) + r3[1].astype(f32)
                + r3[2].astype(f32))


SEMS = (("core_send", (2,)), ("core_recv", (2,)), ("one_send", (2, 3, 6)), ("one_recv", (2, 3, 6)),
        ("two_send", (2, 3, 3)), ("two_recv", (2, 3, 3)), ("three_send", (2, 3, 3)), ("three_recv", (2, 3, 3)),
        ("fwd_send", ()), ("fwd_recv", ()), ("sum_send", ()), ("sum_recv", ()), ("back_send", ()),
        ("back_recv", ()), ("local", (7,)))


def whole_kernel(slot_ref, block_ref, x_ref, dense_ref, label_ref, weight_ref, wide_ref, mid_ref, narrow_ref,
                 in_hbm, out_hbm, bias_in, head_ref, sums_ref, back_ref, total_ref,
                 slots_ref, w_ref, t_ref, in_ref, out_ref, in_t, out_t, vec_ref, col, cols_ref, sg_ref, lg_ref, start, layer,
                 low0, low1, gate0, gate1, stage, bias_ref, owner_mask, place_mask, *rest):
    low = jnp.bfloat16
    f32 = jnp.float32
    projections = (wide_ref, mid_ref, narrow_ref)
    grads, core_bufs, rest = rest[:2], rest[2:4], rest[4:]
    rs_bufs = [[rest[(l * 3 + p) * 6:(l * 3 + p + 1) * 6] for p in range(3)] for l in range(2)]
    sems = {name: sem for (name, _), sem in zip(SEMS, rest[36:-1])}
    sems["round"] = rest[-1]
    at = place()
    me = flat(at)
    sent = []

    def remote(src, dst, ss, rs, to, keep):
        copy = pltpu.make_async_remote_copy(
            src_ref=src, dst_ref=dst, send_sem=ss, recv_sem=rs, device_id=to, device_id_type=MESH)
        copy.start()
        if keep:
            sent.append(copy)
        return copy

    barrier = pltpu.get_barrier_semaphore()

    lines = [[tuple((a + k) % 4 if i == d else a for i, a in enumerate(at[:3])) + at[3:] for k in (1, 2, 3)]
             for d in range(3)]
    near = [at[:3] + (1 - at[3],)] + lines[0] + lines[1] + lines[2]
    for device in near:
        pl.semaphore_signal(barrier, inc=1, device_id=device, device_id_type=MESH)
    loads = []
    for l in range(2):
        loads.append(pltpu.make_async_copy(in_hbm.at[l], in_ref.at[l], sems["local"].at[l]))
        loads.append(pltpu.make_async_copy(out_hbm.at[l], out_ref.at[l], sems["local"].at[2 + l]))
    for load in loads:
        load.start()
    own = pltpu.make_async_copy(x_ref.at[:, columns(me)], slots_ref.at[me], sems["local"].at[4])
    own.start()
    local_sum = jnp.sum(weight_ref[...], axis=1, keepdims=True)
    w_ref[...] = jnp.broadcast_to(local_sum, (1, 128))
    t_ref[me] = jnp.broadcast_to(local_sum, (1, 128))
    ys = [(at[2] + q) % 4 for q in range(4)]
    cores = [at[3], 1 - at[3]]
    xs_now = [(at[0] + q) % 4 for q in range(4)]
    zs_now = [(at[1] + q) % 4 for q in range(4)]

    def to_all(lo, hi, send):
        def some(i, carry):
            xs = [(at[0] + i + q) % 4 for q in range(4)]
            zs = [(at[1] + i // 4 + q) % 4 for q in range(4)]
            for n in range(8):
                to = (xs[TURN_X[n]], zs[TURN_Z[n]], ys[n // 2], cores[n % 2])
                if n == 0:
                    @pl.when(i > 0)
                    def _():
                        send(to)
                else:
                    send(to)
            return carry

        lax.fori_loop(lo, hi, some, 0)

    def send_forward(to):
        remote(x_ref.at[:, columns(flat(to))], slots_ref.at[me], sems["fwd_send"], sems["fwd_recv"], to, False)

    def send_sum(to):
        remote(w_ref, t_ref.at[me], sems["sum_send"], sems["sum_recv"], to, False)

    def send_back(to):
        remote(sg_ref.at[flat(to)], back_ref.at[:, columns(me)], sems["back_send"], sems["back_recv"], to, False)

    def to_known(rounds):
        for x, z, y, c in FORWARD[rounds]:
            send_forward((xs_now[x], zs_now[z], ys[y], cores[c]))

    pl.semaphore_wait(barrier, len(near))
    for d in (2, 1, 0):
        for device in lines[d]:
            pl.semaphore_signal(sems["round"].at[d], inc=1, device_id=device, device_id_type=MESH)
        to_known(2 - d)
        pl.semaphore_wait(sems["round"].at[d], 3)
    to_known(3)


    row = lax.broadcasted_iota(jnp.int32, (TILE, 128), 0)
    lane = lax.broadcasted_iota(jnp.int32, (TILE, 128), 1)
    place_mask[...] = jnp.where(row % SHARE == lane, 1.0, 0.0)
    owner_row = lax.broadcasted_iota(jnp.int32, (OWNERS, TILE), 0)
    owner_lane = lax.broadcasted_iota(jnp.int32, (OWNERS, TILE), 1)
    owner_mask[...] = jnp.where(owner_lane // SHARE == owner_row, 1.0, 0.0).astype(low)
    for g in range(4):
        stage[g, pl.ds(TILE, 8), :] = jnp.zeros((8, 128), f32)
    vec_ref[...] = jnp.zeros(vec_ref.shape, f32)
    vec_ref[pl.ds(0, 2), :] = bias_in[...]
    for i in range(WIDTH // 128):
        vec_ref[2, pl.ds(i * 128, 128)] = head_ref[pl.ds(i * 128, 128)]
    for i in range(WIDTH // 128):
        col[pl.ds(i * 128, 128), :] = vec_ref[:, pl.ds(i * 128, 128)].T
    start[pl.ds(0, 128), :] = dense_ref[...]
    for load in loads:
        load.wait()
    for l in range(2):
        in_t[l] = in_ref[l].T
        out_t[l] = out_ref[l].T
    to_all(0, 16, send_sum)
    own.wait()
    most = slots_ref.at[pl.ds(0, DEVICES - 1)]
    pltpu.make_async_copy(most, most, sems["fwd_recv"]).wait()

    def gather(b, carry):
        cols_ref[pl.ds(pl.multiple_of(b * 16, 16), 16), :] = slots_ref[slot_ref[b]]
        return carry

    lax.fori_loop(0, BLOCKS, gather, 0, unroll=8)
    for n, (which, t, column, width) in enumerate(table_rows()):
        start[pl.ds(128 + n * 128, 128), :] = contract(
            projections[which][t], cols_ref[pl.ds(column, width), :], 0, 0).astype(low)

    hidden0 = contract(in_t[0], start[...], 1, 0).astype(low)

    def tile(i):
        return pl.ds(pl.multiple_of(i * TILE, 16), TILE)

    def forward0(i, carry):
        here = tile(i)
        gate = contract(out_t[0, here, :], hidden0, 1, 0) + col[here, 0:1]
        gate0[here, :] = gate
        s = start[here, :].astype(f32)
        layer[here, :] = (s * gate + s).astype(low)
        return carry

    lax.fori_loop(0, TILES, forward0, 0, unroll=2)
    hidden1 = contract(in_t[1], layer[...], 1, 0).astype(low)

    def forward1(i, logit):
        here = tile(i)
        gate = contract(out_t[1, here, :], hidden1, 1, 0) + col[here, 1:2]
        gate1[here, :] = gate
        last = (start[here, :].astype(f32) * gate + layer[here, :].astype(f32)).astype(low).astype(f32)
        return logit + jnp.sum((col[here, 2:3] * last).reshape(TILE // 8, 8, ROWS), axis=0)

    logit = lax.fori_loop(0, TILES, forward1, jnp.zeros((8, ROWS), f32), unroll=2)
    logit = jnp.sum(logit, axis=0, keepdims=True)
    signal = weight_ref[...] * (jax.nn.sigmoid(logit) - label_ref[...].astype(f32))

    def keep_bias(l, i, gate_grad):
        sums = jnp.sum(gate_grad, axis=1, keepdims=True)
        spread = (place_mask[...] * sums).astype(low)
        bias_ref[l, pl.ds(pl.multiple_of(i * OWNERS, 16), OWNERS), :] = contract(owner_mask[...], spread, 1, 0)

    def backward1(i, carry):
        here = tile(i)
        gate_grad = start[here, :].astype(f32) * (col[here, 2:3] * signal)
        keep_bias(1, i, gate_grad)
        low1[here, :] = gate_grad.astype(low)
        return carry

    lax.fori_loop(0, TILES, backward1, 0, unroll=2)
    grad1 = contract(out_ref[1], low1[...], 1, 0).astype(low)
    bias_row = lax.broadcasted_iota(jnp.int32, (SLOT, 128), 0) == SHARE
    reductions = [
        Reduction(l, at, grads[l], core_bufs[l], rs_bufs[l], sems, remote) for l in range(2)]

    def pack(l, i, in_term, out_term):
        for h in range(2):
            stage[h, pl.ds(0, TILE), :] = in_term[:, h * 128:(h + 1) * 128]
            stage[2 + h, pl.ds(0, TILE), :] = out_term[:, h * 128:(h + 1) * 128]
        for o in range(OWNERS):
            for g in range(4):
                piece = stage[g, pl.ds(SHARE * o, SLOT), :]
                if g == 0:
                    piece = jnp.where(bias_row, bias_ref[l, pl.ds(i * OWNERS + o, 1), :], piece)
                grads[l][i // 2, 2 * (i % 2) + o // 8, (o // 2) % 4, o % 2, pl.ds(g * SLOT, SLOT), :] = (
                    piece.astype(low))

        @pl.when(i > 0)
        def _():
            reductions[l].send_tile(i - 1)

    def backward0(i, carry):
        here = tile(i)
        pack(1, i, contract(layer[here, :], grad1, 1, 1), contract(low1[here, :], hidden1, 1, 1))
        above = col[here, 2:3] * signal
        upstream = above + contract(in_ref[1, here, :], grad1, 1, 0)
        gate_grad = start[here, :].astype(f32) * upstream
        keep_bias(0, i, gate_grad)
        low0[here, :] = gate_grad.astype(low)
        gate0[here, :] = gate1[here, :] * above + gate0[here, :] * upstream + upstream
        return carry

    lax.fori_loop(0, TILES, backward0, 0, unroll=2)
    reductions[1].send_tile(TILES - 1)
    grad0 = contract(out_ref[0], low0[...], 1, 0).astype(low)
    reductions[1].first()

    def finish(i, carry):
        here = tile(i)
        low1[here, :] = (gate0[here, :] + contract(in_ref[0, here, :], grad0, 1, 0)).astype(low)
        return carry

    lax.fori_loop(0, TILES, finish, 0, unroll=2)
    for n, (which, t, column, width) in enumerate(table_rows()):
        lg_ref[pl.ds(column // 16, width // 16)] = contract(
            projections[which][t], low1[pl.ds(128 + n * 128, 128), :], 1, 0).astype(low).reshape(
                width // 16, 16, ROWS)

    def spread(s, carry):
        sg_ref[s] = lg_ref[block_ref[s]]
        return carry

    lax.fori_loop(0, BLOCKS, spread, 0, unroll=8)

    own_back = pltpu.make_async_copy(sg_ref.at[me], back_ref.at[:, columns(me)], sems["local"].at[5])
    own_back.start()
    to_all(0, 5, send_back)

    def terms0(i, carry):
        here = tile(i)
        pack(0, i, contract(start[here, :], grad0, 1, 1), contract(low0[here, :], hidden0, 1, 1))
        return carry

    lax.fori_loop(0, TILES, terms0, 0, unroll=2)
    reductions[0].send_tile(TILES - 1)
    reductions[1].middle()
    to_all(5, 7, send_back)
    reductions[0].first()
    reductions[1].second()
    to_all(7, 10, send_back)
    reductions[0].middle()
    reductions[1].third()
    to_all(10, 13, send_back)
    reductions[0].second()
    reductions[1].last(sums_ref)
    to_all(13, 16, send_back)
    small = t_ref.at[pl.ds(0, DEVICES - 1)]
    pltpu.make_async_copy(small, small, sems["sum_recv"]).wait()
    total_ref[...] = jnp.sum(t_ref[...], axis=0)
    reductions[0].third()
    reductions[0].last(sums_ref)

    own_back.wait()
    for copy in sent:
        copy.wait_send()
    for reduction in reductions:
        reduction.wait_core("core_send")
    pltpu.make_async_copy(small, small, sems["sum_send"]).wait()
    pltpu.make_async_copy(most, most, sems["fwd_send"]).wait()
    pltpu.make_async_copy(most, most, sems["back_send"]).wait()
    pltpu.make_async_copy(most, most, sems["back_recv"]).wait()


def whole(slot_of_block, block_of_slot, pooled, dense, labels, weights, wide, mid, narrow, cross_in, cross_out, bias,
          head):
    vmem = pl.BlockSpec(memory_space=VM)
    smem = pl.BlockSpec(memory_space=pltpu.SMEM)
    hbm = pl.BlockSpec(memory_space=pl.ANY)
    low, f32 = jnp.bfloat16, jnp.float32
    activation = VM((WIDTH, ROWS), low)
    full = VM((WIDTH, ROWS), f32)
    scratch = [
        VM((DEVICES, 16, ROWS), low), VM((1, 128), f32), VM((DEVICES, 1, 128), f32),
        VM((2, WIDTH, 256), low), VM((2, 256, WIDTH), low), VM((2, 256, WIDTH), low), VM((2, WIDTH, 256), low),
        VM((8, WIDTH), f32), VM((WIDTH, 8), f32), VM((2048, ROWS), low), VM((DEVICES, 16, ROWS), low),
        VM((DEVICES, 16, ROWS), low),
        activation, activation, activation, activation, full, full,
        VM((4, TILE + 8, 128), f32), VM((2, DEVICES, 128), f32), VM((OWNERS, TILE), low), VM((TILE, 128), f32),
    ]
    scratch += [VM((4, 4, 4, 2, OWNED, 128), low)] * 2 + [VM((4, 4, 4, OWNED, 128), low)] * 2
    for l in range(2):
        for lo, hi, _ in PARTS[l]:
            n = hi - lo
            scratch += [VM((2, 4, n, 128), low), VM((2, 4, n, 128), low), VM((4, 4, n, 128), low),
                        VM((4, 4, n, 128), low), VM((3, 4, n, 128), low), VM((3, n, 128), low)]
    scratch += [pltpu.SemaphoreType.DMA(shape) if shape else pltpu.SemaphoreType.DMA for _, shape in SEMS]
    scratch.append(pltpu.SemaphoreType.REGULAR((3,)))
    return pl.pallas_call(
        whole_kernel,
        out_shape=(jax.ShapeDtypeStruct((2, OWNED, 128), f32),
                   jax.ShapeDtypeStruct((16, DEVICES * ROWS), low),
                   jax.ShapeDtypeStruct((1, 128), f32)),
        in_specs=[smem, smem, hbm] + [vmem] * 6 + [hbm, hbm, vmem, vmem],
        out_specs=(vmem, vmem, vmem),
        scratch_shapes=scratch,
        compiler_params=pltpu.CompilerParams(
            has_side_effects=True, collective_id=0, vmem_limit_bytes=60 * 1024 * 1024),
        name="whole",
    )(slot_of_block, block_of_slot, pooled, dense, labels, weights, wide, mid, narrow, cross_in, cross_out, bias, head)


PIECES = 2


def post_kernel(back_ref, sums_ref, total_ref, pooled_ref, in_ref, out_ref, bias_ref):
    scale = BATCH_ROWS / total_ref[...]
    many = back_ref.shape[1] // 128

    def move(j, carry):
        part = back_ref[:, pl.ds(pl.multiple_of(j * 1024, 1024), 1024)].astype(jnp.float32) * wide
        pooled_ref[:, pl.ds(pl.multiple_of(j * 8, 8), 8), :] = pltpu.einshape("c(jl)->cjl", part, j=8, l=128)
        return carry

    wide = jnp.tile(scale, (1, 8))
    lax.fori_loop(0, many // 8, move, 0, unroll=2)

    @pl.when(pl.program_id(0) == 0)
    def _():
        for l in range(2):
            for h in range(2):
                in_ref[:, h, l, :] = sums_ref[l, pl.ds(h * SLOT, SHARE), :] * scale
                out_ref[:, h, l, :] = sums_ref[l, pl.ds((2 + h) * SLOT, SHARE), :] * scale
            bias_ref[pl.ds(l, 1), :] = (sums_ref[l, pl.ds(SHARE, 1), :] * scale)[:, :SHARE]


def post(returned, sums, total):
    f32 = jnp.float32
    many = DEVICES * ROWS // 128
    once = lambda shape: pl.BlockSpec(shape, lambda i: (0,) * len(shape))
    return pl.pallas_call(
        post_kernel,
        grid=(PIECES,),
        out_shape=(jax.ShapeDtypeStruct((BLOCK_WIDTH, many, 128), f32),
                   jax.ShapeDtypeStruct((SHARE, 2, 2, 128), f32),
                   jax.ShapeDtypeStruct((SHARE, 2, 2, 128), f32),
                   jax.ShapeDtypeStruct((2, SHARE), f32)),
        in_specs=[pl.BlockSpec((BLOCK_WIDTH, DEVICES * ROWS // PIECES), lambda i: (0, i)),
                  once((2, OWNED, 128)), once((1, 128))],
        out_specs=(pl.BlockSpec((BLOCK_WIDTH, many // PIECES, 128), lambda i: (0, i, 0)),
                   once((SHARE, 2, 2, 128)), once((SHARE, 2, 2, 128)), once((2, SHARE))),
        name="post",
    )(returned, sums, total)


def unpacked(rows):
    return jnp.transpose(rows, (2, 0, 1, 3)).reshape(2, SHARE, 256)


def body(
    pooled,
    slot_of_block,
    dense_part,
    labels,
    sample_weight,
    proj_wide,
    proj_mid,
    proj_narrow,
    cross_in,
    cross_out,
    cross_bias,
    head_weight,
):
    numbers = jnp.arange(BLOCKS, dtype=jnp.int32)
    block_of_slot = jnp.max(jnp.where(slot_of_block[None, :] == numbers[:, None], numbers[None, :], 0), 1)
    sums, returned, total = whole(
        slot_of_block,
        block_of_slot,
        pooled.reshape(BLOCK_WIDTH, BATCH_ROWS),
        dense_part,
        labels[None],
        sample_weight[None],
        proj_wide,
        proj_mid,
        proj_narrow,
        cross_in,
        cross_out,
        cross_bias,
        head_weight,
    )
    pooled_grad, grad_in, grad_out, grad_bias = post(returned, sums, total)
    return (
        pooled_grad.reshape(BLOCK_WIDTH, 1, BATCH_ROWS),
        unpacked(grad_in),
        jnp.swapaxes(unpacked(grad_out), 1, 2),
        grad_bias,
    )


def solution(mesh):
    finer = Mesh(mesh.devices.reshape(4, 4, 4, mesh.shape["rep"]), ("dp_0", "dp_1", "dp_2", "rep"))
    return jax.shard_map(
        body,
        mesh=finer,
        in_specs=(
            P(None, DP_REP, None),
            P(),
            P(None, DP_REP),
            P(DP_REP),
            P(DP_REP),
            P(),
            P(),
            P(),
            P(),
            P(),
            P(),
            P(),
        ),
        out_specs=(
            P(None, DP_REP, None),
            P(None, DP_REP, None),
            P(None, None, DP_REP),
            P(None, DP_REP),
        ),
        check_vma=False,
    )
```

```python
import jax
import jax.numpy as jnp
from jax import lax
from jax.experimental import pallas as pl
from jax.experimental.pallas import tpu as pltpu
from jax.sharding import Mesh
from jax.sharding import PartitionSpec as P

BLOCK_WIDTH = 16
BLOCKS = 128
BATCH_ROWS = 32768
DP_REP = ("dp_0", "dp_1", "dp_2", "rep")
AXES = DP_REP
MESH = pl.DeviceIdType.MESH
DEVICES = 128
ROWS = 256
TILE = 432
TILES = 8
OWNERS = 16
WIDTH = 3456
SHARE = 27
SLOT = 32
OWNED = 128
CLOSE = 112
VM = pltpu.VMEM
PARTS = (
    ((0, 32, (0, 1, 2)), (32, 64, (1, 2, 0)), (64, 112, (2, 0, 1))),
    ((0, 48, (0, 1, 2)), (48, 96, (1, 2, 0)), (96, 128, (2, 0, 1))),
)


def known_after(x, z, y, c):
    others = (x != 0) + (c != 0)
    if others + (z != 0) + (y != 0) == 1:
        return 0
    if not z:
        return 1 if y and others == 1 else 3
    return 2 if others < 2 else 3


def sends_of(rounds):
    steps = [((k // 32), (k // 8) % 4, (k // 2) % 4, k % 2) for k in [(37 * i) % 128 for i in range(1, 128)]]
    steps = [step for step in steps if (known_after(*step) if sum(map(bool, step)) != 2 or not (
        step[1] and step[2]) else 1) == rounds]
    return sorted(steps, key=lambda step: -sum(min(v, 4 - v) for v in step[:3]))


FORWARD = [sends_of(rounds) for rounds in range(4)]
TURN_X = (0, 1, 2, 3, 1, 2, 3, 0)
TURN_Z = (0, 2, 1, 3, 3, 1, 0, 2)
HALVES = (pl.ds(0, 2), pl.ds(2, 2))


def place():
    return tuple(lax.axis_index(a) for a in AXES)


def flat(at):
    return ((at[0] * 4 + at[1]) * 4 + at[2]) * 2 + at[3]


def columns(device):
    return pl.ds(pl.multiple_of(device * ROWS, ROWS), ROWS)


def contract(a, b, da, db):
    return lax.dot_general(a, b, (((da,), (db,)), ((), ())), preferred_element_type=jnp.float32)


def table_rows():
    rows = []
    column = 0
    for which, (count, width) in enumerate(((6, 256), (4, 64), (16, 16))):
        for t in range(count):
            rows.append((which, t, column, width))
            column += width
    return rows


def sub(ref, chosen, tail):
    return ref.at[tuple(chosen.get(d, slice(None)) for d in range(3)) + tail]


class Reduction:
    def __init__(self, layer, at, grads, core_buf, bufs, sems, remote):
        self.layer, self.at, self.core = layer, at, at[3]
        self.grads, self.core_buf, self.bufs, self.sems = grads, core_buf, bufs, sems
        self.remote = remote
        self.one, self.two, self.three, self.kept = {}, {}, {}, {}

    def moved(self, d, k):
        return tuple((a + k) % 4 if i == d else a for i, a in enumerate(self.at[:3])) + (self.core,)

    def send_tile(self, i):
        there = pl.ds(2 * (i % 2), 2)
        self.remote(
            self.grads.at[i // 2, there, :, 1 - self.core], self.core_buf.at[i // 2, there],
            self.sems["core_send"].at[self.layer], self.sems["core_recv"].at[self.layer],
            self.at[:3] + (1 - self.core,), False)

    def wait_core(self, which):
        pltpu.make_async_copy(self.core_buf, self.core_buf, self.sems[which].at[self.layer]).wait()

    def step(self, which, p, n, src, dst, d, k):
        return self.remote(src, dst, self.sems[which + "_send"].at[self.layer, p, n],
                           self.sems[which + "_recv"].at[self.layer, p, n], self.moved(d, k), True)

    def first(self):
        self.wait_core("core_recv")

        def fold(b, carry):
            x, z = b // 4, b % 4
            for y in range(4):
                self.core_buf[x, z, y] = self.core_buf[x, z, y] + self.grads[x, z, y, self.core]
            return carry

        lax.fori_loop(0, 16, fold, 0)
        for p, (lo, hi, (d, _, _)) in enumerate(PARTS[self.layer]):
            tail = (pl.ds(lo, hi - lo), slice(None))
            for k in range(4):
                self.kept[p, k] = sub(self.core_buf, {d: (self.at[d] + k) % 4}, tail)
            ra, rb = self.bufs[p][:2]
            self.one[p, 0] = self.step("one", p, 0, self.kept[p, 2].at[HALVES[0]], ra, d, 1)
            self.one[p, 1] = self.step("one", p, 1, self.kept[p, 2].at[HALVES[1]], rb, d, 3)
        for p, (lo, hi, (d, _, _)) in enumerate(PARTS[self.layer]):
            rp, rm = self.bufs[p][2:4]
            self.one[p, 2] = self.step(
                "one", p, 2, self.kept[p, 1].at[HALVES[1]], rp.at[HALVES[1]], d, 1)
            self.one[p, 3] = self.step(
                "one", p, 3, self.kept[p, 3].at[HALVES[0]], rm.at[HALVES[0]], d, 3)

    def middle(self):
        for p, (lo, hi, (d, _, _)) in enumerate(PARTS[self.layer]):
            ra, rb, rp, rm = self.bufs[p][:4]
            self.one[p, 0].wait_recv()
            up = self.kept[p, 1].at[HALVES[0]]
            up[...] = up[...] + ra[...]
            self.one[p, 4] = self.step("one", p, 4, up, rp.at[HALVES[0]], d, 1)
            self.one[p, 1].wait_recv()
            down = self.kept[p, 3].at[HALVES[1]]
            down[...] = down[...] + rb[...]
            self.one[p, 5] = self.step("one", p, 5, down, rm.at[HALVES[1]], d, 3)

    def second(self):
        f32 = jnp.float32
        for p, (lo, hi, (d, e, f)) in enumerate(PARTS[self.layer]):
            rp, rm, r2 = self.bufs[p][2:5]
            for n in range(2, 6):
                self.one[p, n].wait_recv()
            total = self.kept[p, 0]
            for i in range(4):
                total[i] = (total[i].astype(f32) + rp[i].astype(f32) + rm[i].astype(f32)).astype(jnp.bfloat16)
            for k in (2, 1, 3):
                self.two[p, k] = self.step(
                    "two", p, k - 1, self.pick(p, {e: (self.at[e] + k) % 4}), r2.at[k - 1], e, k)

    def pick(self, p, chosen):
        d = PARTS[self.layer][p][2][0]
        return self.kept[p, 0].at[tuple(chosen.get(i, slice(None)) for i in range(3) if i != d)]

    def third(self):
        f32 = jnp.float32
        self.held = {}
        for p, (lo, hi, (d, e, f)) in enumerate(PARTS[self.layer]):
            r2, r3 = self.bufs[p][4:6]
            for k in (1, 2, 3):
                self.two[p, k].wait_recv()
            mine = self.pick(p, {e: self.at[e]})
            mine[...] = (mine[...].astype(f32) + r2[0].astype(f32) + r2[1].astype(f32)
                         + r2[2].astype(f32)).astype(jnp.bfloat16)
            self.held[p] = mine
            for k in (2, 1, 3):
                self.three[p, k] = self.step(
                    "three", p, k - 1, mine.at[(self.at[f] + k) % 4], r3.at[k - 1], f, k)

    def last(self, out_ref):
        f32 = jnp.float32
        for p, (lo, hi, (d, e, f)) in enumerate(PARTS[self.layer]):
            r3 = self.bufs[p][5]
            for k in (1, 2, 3):
                self.three[p, k].wait_recv()
            out_ref[self.layer, pl.ds(lo, hi - lo), :] = (
                self.held[p].at[self.at[f]][...].astype(f32) + r3[0].astype(f32) + r3[1].astype(f32)
                + r3[2].astype(f32))


SEMS = (("core_send", (2,)), ("core_recv", (2,)), ("one_send", (2, 3, 6)), ("one_recv", (2, 3, 6)),
        ("two_send", (2, 3, 3)), ("two_recv", (2, 3, 3)), ("three_send", (2, 3, 3)), ("three_recv", (2, 3, 3)),
        ("fwd_send", ()), ("fwd_recv", ()), ("sum_send", ()), ("sum_recv", ()), ("back_send", ()),
        ("back_recv", ()), ("local", (13,)))


def whole_kernel(slot_ref, block_ref, x_ref, dense_hbm, label_ref, weight_ref, wide_hbm, mid_hbm, narrow_hbm,
                 in_hbm, out_hbm, bias_hbm, head_hbm, sums_ref, back_ref, total_ref,
                 dense_ref, wide_ref, mid_ref, narrow_ref, bias_in, head_ref, slots_ref, w_ref, t_ref, in_ref, out_ref, in_t, out_t, vec_ref, col, cols_ref, sg_ref, lg_ref, start, layer,
                 low0, low1, gate0, gate1, stage, bias_ref, owner_mask, place_mask, close, *rest):
    low = jnp.bfloat16
    f32 = jnp.float32
    projections = (wide_ref, mid_ref, narrow_ref)
    grads, core_bufs, rest = rest[:2], rest[2:4], rest[4:]
    rs_bufs = [[rest[(l * 3 + p) * 6:(l * 3 + p + 1) * 6] for p in range(3)] for l in range(2)]
    sems = {name: sem for (name, _), sem in zip(SEMS, rest[36:-1])}
    sems["round"] = rest[-1]
    at = place()
    me = flat(at)
    sent = []

    def remote(src, dst, ss, rs, to, keep):
        copy = pltpu.make_async_remote_copy(
            src_ref=src, dst_ref=dst, send_sem=ss, recv_sem=rs, device_id=to, device_id_type=MESH)
        copy.start()
        if keep:
            sent.append(copy)
        return copy

    barrier = pltpu.get_barrier_semaphore()

    lines = [[tuple((a + k) % 4 if i == d else a for i, a in enumerate(at[:3])) + at[3:] for k in (1, 2, 3)]
             for d in range(3)]
    near = [at[:3] + (1 - at[3],)] + lines[0] + lines[1] + lines[2]
    for device in near:
        pl.semaphore_signal(barrier, inc=1, device_id=device, device_id_type=MESH)
    loads = []
    for l in range(2):
        loads.append(pltpu.make_async_copy(in_hbm.at[l], in_ref.at[l], sems["local"].at[l]))
        loads.append(pltpu.make_async_copy(out_hbm.at[l], out_ref.at[l], sems["local"].at[2 + l]))
    small_loads = [
        pltpu.make_async_copy(src, dst, sems["local"].at[7 + n]) for n, (src, dst) in enumerate((
            (dense_hbm, dense_ref), (wide_hbm, wide_ref), (mid_hbm, mid_ref), (narrow_hbm, narrow_ref),
            (bias_hbm, bias_in), (head_hbm, head_ref)))]
    for load in small_loads + loads:
        load.start()
    own = pltpu.make_async_copy(x_ref.at[:, columns(me)], slots_ref.at[me], sems["local"].at[4])
    own.start()
    local_sum = jnp.sum(weight_ref[...], axis=1, keepdims=True)
    w_ref[...] = jnp.broadcast_to(local_sum, (1, 128))
    t_ref[me] = jnp.broadcast_to(local_sum, (1, 128))
    ys = [(at[2] + q) % 4 for q in range(4)]
    cores = [at[3], 1 - at[3]]
    xs_now = [(at[0] + q) % 4 for q in range(4)]
    zs_now = [(at[1] + q) % 4 for q in range(4)]

    def to_all(lo, hi, send):
        def some(i, carry):
            xs = [(at[0] + i + q) % 4 for q in range(4)]
            zs = [(at[1] + i // 4 + q) % 4 for q in range(4)]
            for n in range(8):
                to = (xs[TURN_X[n]], zs[TURN_Z[n]], ys[n // 2], cores[n % 2])
                if n == 0:
                    @pl.when(i > 0)
                    def _():
                        send(to)
                else:
                    send(to)
            return carry

        lax.fori_loop(lo, hi, some, 0)

    def send_forward(to):
        remote(x_ref.at[:, columns(flat(to))], slots_ref.at[me], sems["fwd_send"], sems["fwd_recv"], to, False)

    def send_sum(to):
        remote(w_ref, t_ref.at[me], sems["sum_send"], sems["sum_recv"], to, False)

    def send_back(to):
        remote(sg_ref.at[flat(to)], back_ref.at[:, columns(me)], sems["back_send"], sems["back_recv"], to, False)

    def to_known(rounds):
        for x, z, y, c in FORWARD[rounds]:
            send_forward((xs_now[x], zs_now[z], ys[y], cores[c]))

    pl.semaphore_wait(barrier, len(near))
    for d in (2, 1, 0):
        for device in lines[d]:
            pl.semaphore_signal(sems["round"].at[d], inc=1, device_id=device, device_id_type=MESH)
        to_known(2 - d)
        pl.semaphore_wait(sems["round"].at[d], 3)
    to_known(3)


    row = lax.broadcasted_iota(jnp.int32, (TILE, 128), 0)
    lane = lax.broadcasted_iota(jnp.int32, (TILE, 128), 1)
    place_mask[...] = jnp.where(row % SHARE == lane, 1.0, 0.0)
    owner_row = lax.broadcasted_iota(jnp.int32, (OWNERS, TILE), 0)
    owner_lane = lax.broadcasted_iota(jnp.int32, (OWNERS, TILE), 1)
    owner_mask[...] = jnp.where(owner_lane // SHARE == owner_row, 1.0, 0.0).astype(low)
    for g in range(4):
        stage[g, pl.ds(TILE, 8), :] = jnp.zeros((8, 128), f32)
    for load in small_loads:
        load.wait()
    vec_ref[...] = jnp.zeros(vec_ref.shape, f32)
    vec_ref[pl.ds(0, 2), :] = bias_in[...]
    for i in range(WIDTH // 128):
        vec_ref[2, pl.ds(i * 128, 128)] = head_ref[pl.ds(i * 128, 128)]
    for i in range(WIDTH // 128):
        col[pl.ds(i * 128, 128), :] = vec_ref[:, pl.ds(i * 128, 128)].T
    start[pl.ds(0, 128), :] = dense_ref[...]
    for load in loads:
        load.wait()
    for l in range(2):
        in_t[l] = in_ref[l].T
        out_t[l] = out_ref[l].T
    to_all(0, 16, send_sum)
    own.wait()
    most = slots_ref.at[pl.ds(0, DEVICES - 1)]
    pltpu.make_async_copy(most, most, sems["fwd_recv"]).wait()

    def gather(b, carry):
        cols_ref[pl.ds(pl.multiple_of(b * 16, 16), 16), :] = slots_ref[slot_ref[b]]
        return carry

    lax.fori_loop(0, BLOCKS, gather, 0, unroll=8)
    for n, (which, t, column, width) in enumerate(table_rows()):
        start[pl.ds(128 + n * 128, 128), :] = contract(
            projections[which][t], cols_ref[pl.ds(column, width), :], 0, 0).astype(low)

    hidden0 = contract(in_t[0], start[...], 1, 0).astype(low)

    def tile(i):
        return pl.ds(pl.multiple_of(i * TILE, 16), TILE)

    def forward0(i, carry):
        here = tile(i)
        gate = contract(out_t[0, here, :], hidden0, 1, 0) + col[here, 0:1]
        gate0[here, :] = gate
        s = start[here, :].astype(f32)
        layer[here, :] = (s * gate + s).astype(low)
        return carry

    lax.fori_loop(0, TILES, forward0, 0, unroll=4)
    hidden1 = contract(in_t[1], layer[...], 1, 0).astype(low)

    def forward1(i, logit):
        here = tile(i)
        gate = contract(out_t[1, here, :], hidden1, 1, 0) + col[here, 1:2]
        gate1[here, :] = gate
        last = (start[here, :].astype(f32) * gate + layer[here, :].astype(f32)).astype(low).astype(f32)
        return logit + jnp.sum((col[here, 2:3] * last).reshape(TILE // 8, 8, ROWS), axis=0)

    logit = lax.fori_loop(0, TILES, forward1, jnp.zeros((8, ROWS), f32), unroll=4)
    logit = jnp.sum(logit, axis=0, keepdims=True)
    signal = weight_ref[...] * (jax.nn.sigmoid(logit) - label_ref[...].astype(f32))

    def keep_bias(l, i, gate_grad):
        sums = jnp.sum(gate_grad, axis=1, keepdims=True)
        spread = (place_mask[...] * sums).astype(low)
        bias_ref[l, pl.ds(pl.multiple_of(i * OWNERS, 16), OWNERS), :] = contract(owner_mask[...], spread, 1, 0)

    def backward1(i, carry):
        here = tile(i)
        gate_grad = start[here, :].astype(f32) * (col[here, 2:3] * signal)
        keep_bias(1, i, gate_grad)
        low1[here, :] = gate_grad.astype(low)
        return carry

    lax.fori_loop(0, TILES, backward1, 0, unroll=4)
    grad1 = contract(out_ref[1], low1[...], 1, 0).astype(low)
    bias_row = lax.broadcasted_iota(jnp.int32, (SLOT, 128), 0) == SHARE
    reductions = [
        Reduction(l, at, grads[l], core_bufs[l], rs_bufs[l], sems, remote) for l in range(2)]

    def pack(l, i, in_term, out_term):
        for h in range(2):
            stage[h, pl.ds(0, TILE), :] = in_term[:, h * 128:(h + 1) * 128]
            stage[2 + h, pl.ds(0, TILE), :] = out_term[:, h * 128:(h + 1) * 128]
        for o in range(OWNERS):
            block = (i // 2, 2 * (i % 2) + o // 8, (o // 2) % 4, o % 2)
            if l == 0:
                for g in range(4):
                    close[o % 4, pl.ds(SHARE * g, SLOT), :] = stage[g, pl.ds(SHARE * o, SLOT), :]
                close[o % 4, pl.ds(4 * SHARE, 1), :] = bias_ref[l, pl.ds(i * OWNERS + o, 1), :]
                grads[l][block] = close[o % 4, pl.ds(0, CLOSE), :].astype(low)
                continue
            for g in range(4):
                piece = stage[g, pl.ds(SHARE * o, SLOT), :]
                if g == 0:
                    piece = jnp.where(bias_row, bias_ref[l, pl.ds(i * OWNERS + o, 1), :], piece)
                grads[l][block + (pl.ds(g * SLOT, SLOT), slice(None))] = (
                    piece.astype(low))

        @pl.when(i > 0)
        def _():
            reductions[l].send_tile(i - 1)

    def terms1(i, carry):
        here = tile(i)
        pack(1, i, contract(layer[here, :], grad1, 1, 1), contract(low1[here, :], hidden1, 1, 1))
        return carry

    lax.fori_loop(0, TILES, terms1, 0, unroll=2)
    reductions[1].send_tile(TILES - 1)
    reductions[1].first()

    def backward0(i, carry):
        here = tile(i)
        above = col[here, 2:3] * signal
        upstream = above + contract(in_ref[1, here, :], grad1, 1, 0)
        gate_grad = start[here, :].astype(f32) * upstream
        keep_bias(0, i, gate_grad)
        low0[here, :] = gate_grad.astype(low)
        gate0[here, :] = gate1[here, :] * above + gate0[here, :] * upstream + upstream
        return carry

    lax.fori_loop(0, TILES, backward0, 0, unroll=2)
    grad0 = contract(out_ref[0], low0[...], 1, 0).astype(low)
    reductions[1].middle()

    def finish(i, carry):
        here = tile(i)
        low1[here, :] = (gate0[here, :] + contract(in_ref[0, here, :], grad0, 1, 0)).astype(low)
        return carry

    lax.fori_loop(0, TILES, finish, 0, unroll=4)
    for n, (which, t, column, width) in enumerate(table_rows()):
        lg_ref[pl.ds(column // 16, width // 16)] = contract(
            projections[which][t], low1[pl.ds(128 + n * 128, 128), :], 1, 0).astype(low).reshape(
                width // 16, 16, ROWS)

    def spread(s, carry):
        sg_ref[s] = lg_ref[block_ref[s]]
        return carry

    lax.fori_loop(0, BLOCKS, spread, 0, unroll=8)

    own_back = pltpu.make_async_copy(sg_ref.at[me], back_ref.at[:, columns(me)], sems["local"].at[5])
    own_back.start()
    def terms0(i, carry):
        here = tile(i)
        pack(0, i, contract(start[here, :], grad0, 1, 1), contract(low0[here, :], hidden0, 1, 1))
        return carry

    to_all(0, 5, send_back)
    lax.fori_loop(0, TILES, terms0, 0, unroll=2)
    reductions[0].send_tile(TILES - 1)
    reductions[1].second()
    to_all(5, 7, send_back)
    reductions[0].first()
    reductions[1].third()
    to_all(7, 10, send_back)
    reductions[0].middle()
    reductions[1].last(sums_ref)
    to_all(10, 13, send_back)
    reductions[0].second()
    to_all(13, 16, send_back)
    small = t_ref.at[pl.ds(0, DEVICES - 1)]
    pltpu.make_async_copy(small, small, sems["sum_recv"]).wait()
    total_ref[...] = jnp.sum(t_ref[...], axis=0)
    reductions[0].third()
    reductions[0].last(sums_ref)

    own_back.wait()
    for copy in sent:
        copy.wait_send()
    for reduction in reductions:
        reduction.wait_core("core_send")
    pltpu.make_async_copy(small, small, sems["sum_send"]).wait()
    pltpu.make_async_copy(most, most, sems["fwd_send"]).wait()
    pltpu.make_async_copy(most, most, sems["back_send"]).wait()
    pltpu.make_async_copy(most, most, sems["back_recv"]).wait()


def whole(slot_of_block, block_of_slot, pooled, dense, labels, weights, wide, mid, narrow, cross_in, cross_out, bias,
          head):
    vmem = pl.BlockSpec(memory_space=VM)
    smem = pl.BlockSpec(memory_space=pltpu.SMEM)
    hbm = pl.BlockSpec(memory_space=pl.ANY)
    low, f32 = jnp.bfloat16, jnp.float32
    activation = VM((WIDTH, ROWS), low)
    full = VM((WIDTH, ROWS), f32)
    scratch = [
        VM((128, ROWS), low), VM(wide.shape, low), VM(mid.shape, low), VM(narrow.shape, low), VM(bias.shape, f32),
        VM(head.shape, f32),
        VM((DEVICES, 16, ROWS), low), VM((1, 128), f32), VM((DEVICES, 1, 128), f32),
        VM((2, WIDTH, 256), low), VM((2, 256, WIDTH), low), VM((2, 256, WIDTH), low), VM((2, WIDTH, 256), low),
        VM((8, WIDTH), f32), VM((WIDTH, 8), f32), VM((2048, ROWS), low), VM((DEVICES, 16, ROWS), low),
        VM((DEVICES, 16, ROWS), low),
        activation, activation, activation, activation, full, full,
        VM((4, TILE + 8, 128), f32), VM((2, DEVICES, 128), f32), VM((OWNERS, TILE), low), VM((TILE, 128), f32),
        VM((4, 120, 128), f32),
    ]
    scratch += [VM((4, 4, 4, 2, n, 128), low) for n in (CLOSE, OWNED)]
    scratch += [VM((4, 4, 4, n, 128), low) for n in (CLOSE, OWNED)]
    for l in range(2):
        for lo, hi, _ in PARTS[l]:
            n = hi - lo
            scratch += [VM((2, 4, n, 128), low), VM((2, 4, n, 128), low), VM((4, 4, n, 128), low),
                        VM((4, 4, n, 128), low), VM((3, 4, n, 128), low), VM((3, n, 128), low)]
    scratch += [pltpu.SemaphoreType.DMA(shape) if shape else pltpu.SemaphoreType.DMA for _, shape in SEMS]
    scratch.append(pltpu.SemaphoreType.REGULAR((3,)))
    return pl.pallas_call(
        whole_kernel,
        out_shape=(jax.ShapeDtypeStruct((2, OWNED, 128), f32),
                   jax.ShapeDtypeStruct((16, DEVICES * ROWS), low),
                   jax.ShapeDtypeStruct((1, 128), f32)),
        in_specs=[smem, smem, hbm, hbm, vmem, vmem] + [hbm] * 7,
        out_specs=(vmem, vmem, vmem),
        scratch_shapes=scratch,
        compiler_params=pltpu.CompilerParams(
            has_side_effects=True, collective_id=0, vmem_limit_bytes=60 * 1024 * 1024),
        name="whole",
    )(slot_of_block, block_of_slot, pooled, dense, labels, weights, wide, mid, narrow, cross_in, cross_out, bias, head)


PIECES = 2


def post_kernel(back_ref, sums_ref, total_ref, pooled_ref, in_ref, out_ref, bias_ref):
    scale = BATCH_ROWS / total_ref[...]
    many = back_ref.shape[1] // 128

    def move(j, carry):
        part = back_ref[:, pl.ds(pl.multiple_of(j * 1024, 1024), 1024)].astype(jnp.float32) * wide
        pooled_ref[:, pl.ds(pl.multiple_of(j * 8, 8), 8), :] = pltpu.einshape("c(jl)->cjl", part, j=8, l=128)
        return carry

    wide = jnp.tile(scale, (1, 8))
    lax.fori_loop(0, many // 8, move, 0, unroll=2)

    @pl.when(pl.program_id(0) == 0)
    def _():
        for l in range(2):
            for h in range(2):
                step = (SHARE, SLOT)[l]
                in_ref[:, h, l, :] = sums_ref[l, pl.ds(h * step, SHARE), :] * scale
                out_ref[:, h, l, :] = sums_ref[l, pl.ds((2 + h) * step, SHARE), :] * scale
            bias_ref[pl.ds(l, 1), :] = (sums_ref[l, pl.ds((4 * SHARE, SHARE)[l], 1), :] * scale)[:, :SHARE]


def post(returned, sums, total):
    f32 = jnp.float32
    many = DEVICES * ROWS // 128
    once = lambda shape: pl.BlockSpec(shape, lambda i: (0,) * len(shape))
    return pl.pallas_call(
        post_kernel,
        grid=(PIECES,),
        out_shape=(jax.ShapeDtypeStruct((BLOCK_WIDTH, many, 128), f32),
                   jax.ShapeDtypeStruct((SHARE, 2, 2, 128), f32),
                   jax.ShapeDtypeStruct((SHARE, 2, 2, 128), f32),
                   jax.ShapeDtypeStruct((2, SHARE), f32)),
        in_specs=[pl.BlockSpec((BLOCK_WIDTH, DEVICES * ROWS // PIECES), lambda i: (0, i)),
                  once((2, OWNED, 128)), once((1, 128))],
        out_specs=(pl.BlockSpec((BLOCK_WIDTH, many // PIECES, 128), lambda i: (0, i, 0)),
                   once((SHARE, 2, 2, 128)), once((SHARE, 2, 2, 128)), once((2, SHARE))),
        name="post",
    )(returned, sums, total)


def unpacked(rows):
    return jnp.transpose(rows, (2, 0, 1, 3)).reshape(2, SHARE, 256)


def body(
    pooled,
    slot_of_block,
    dense_part,
    labels,
    sample_weight,
    proj_wide,
    proj_mid,
    proj_narrow,
    cross_in,
    cross_out,
    cross_bias,
    head_weight,
):
    numbers = jnp.arange(BLOCKS, dtype=jnp.int32)
    block_of_slot = jnp.max(jnp.where(slot_of_block[None, :] == numbers[:, None], numbers[None, :], 0), 1)
    sums, returned, total = whole(
        slot_of_block,
        block_of_slot,
        pooled.reshape(BLOCK_WIDTH, BATCH_ROWS),
        dense_part,
        labels[None],
        sample_weight[None],
        proj_wide,
        proj_mid,
        proj_narrow,
        cross_in,
        cross_out,
        cross_bias,
        head_weight,
    )
    pooled_grad, grad_in, grad_out, grad_bias = post(returned, sums, total)
    return (
        pooled_grad.reshape(BLOCK_WIDTH, 1, BATCH_ROWS),
        unpacked(grad_in),
        jnp.swapaxes(unpacked(grad_out), 1, 2),
        grad_bias,
    )


def solution(mesh):
    finer = Mesh(mesh.devices.reshape(4, 4, 4, mesh.shape["rep"]), ("dp_0", "dp_1", "dp_2", "rep"))
    return jax.shard_map(
        body,
        mesh=finer,
        in_specs=(
            P(None, DP_REP, None),
            P(),
            P(None, DP_REP),
            P(DP_REP),
            P(DP_REP),
            P(),
            P(),
            P(),
            P(),
            P(),
            P(),
            P(),
        ),
        out_specs=(
            P(None, DP_REP, None),
            P(None, DP_REP, None),
            P(None, None, DP_REP),
            P(None, DP_REP),
        ),
        check_vma=False,
    )
```

```python
import jax
import jax.numpy as jnp
from jax import lax
from jax.experimental import pallas as pl
from jax.experimental.pallas import tpu as pltpu
from jax.sharding import Mesh
from jax.sharding import PartitionSpec as P

BLOCK_WIDTH = 16
BLOCKS = 128
BATCH_ROWS = 32768
DP_REP = ("dp_0", "dp_1", "dp_2", "rep")
AXES = DP_REP
MESH = pl.DeviceIdType.MESH
DEVICES = 128
ROWS = 256
TILE = 432
TILES = 8
OWNERS = 16
WIDTH = 3456
SHARE = 27
SLOT = 32
OWNED = 128
CLOSE = 112
VM = pltpu.VMEM
PARTS = (
    ((0, 32, (0, 1, 2)), (32, 64, (1, 2, 0)), (64, 112, (2, 0, 1))),
    ((0, 48, (0, 1, 2)), (48, 96, (1, 2, 0)), (96, 128, (2, 0, 1))),
)


def known_after(x, z, y, c):
    others = (x != 0) + (c != 0)
    if others + (z != 0) + (y != 0) == 1:
        return 0
    if not z:
        return 1 if y and others == 1 else 3
    return 2 if others < 2 else 3


def sends_of(rounds):
    steps = [((k // 32), (k // 8) % 4, (k // 2) % 4, k % 2) for k in [(37 * i) % 128 for i in range(1, 128)]]
    steps = [step for step in steps if (known_after(*step) if sum(map(bool, step)) != 2 or not (
        step[1] and step[2]) else 1) == rounds]
    return sorted(steps, key=lambda step: -sum(min(v, 4 - v) for v in step[:3]))


FORWARD = [sends_of(rounds) for rounds in range(4)]
TURN_X = (0, 1, 2, 3, 1, 2, 3, 0)
TURN_Z = (0, 2, 1, 3, 3, 1, 0, 2)
HALVES = (pl.ds(0, 2), pl.ds(2, 2))


def place():
    return tuple(lax.axis_index(a) for a in AXES)


def flat(at):
    return ((at[0] * 4 + at[1]) * 4 + at[2]) * 2 + at[3]


def columns(device):
    return pl.ds(pl.multiple_of(device * ROWS, ROWS), ROWS)


def contract(a, b, da, db):
    return lax.dot_general(a, b, (((da,), (db,)), ((), ())), preferred_element_type=jnp.float32)


def table_rows():
    rows = []
    column = 0
    for which, (count, width) in enumerate(((6, 256), (4, 64), (16, 16))):
        for t in range(count):
            rows.append((which, t, column, width))
            column += width
    return rows


def sub(ref, chosen, tail):
    return ref.at[tuple(chosen.get(d, slice(None)) for d in range(3)) + tail]


class Reduction:
    def __init__(self, layer, at, grads, core_buf, bufs, sems, remote):
        self.layer, self.at, self.core = layer, at, at[3]
        self.grads, self.core_buf, self.bufs, self.sems = grads, core_buf, bufs, sems
        self.remote = remote
        self.one, self.two, self.three, self.kept = {}, {}, {}, {}

    def moved(self, d, k):
        return tuple((a + k) % 4 if i == d else a for i, a in enumerate(self.at[:3])) + (self.core,)

    def send_tile(self, i):
        there = pl.ds(2 * (i % 2), 2)
        self.remote(
            self.grads.at[i // 2, there, :, 1 - self.core], self.core_buf.at[i // 2, there],
            self.sems["core_send"].at[self.layer], self.sems["core_recv"].at[self.layer],
            self.at[:3] + (1 - self.core,), False)

    def wait_core(self, which):
        pltpu.make_async_copy(self.core_buf, self.core_buf, self.sems[which].at[self.layer]).wait()

    def step(self, which, p, n, src, dst, d, k):
        return self.remote(src, dst, self.sems[which + "_send"].at[self.layer, p, n],
                           self.sems[which + "_recv"].at[self.layer, p, n], self.moved(d, k), True)

    def first(self):
        self.wait_core("core_recv")

        def fold(b, carry):
            x, z = b // 4, b % 4
            for y in range(4):
                self.core_buf[x, z, y] = self.core_buf[x, z, y] + self.grads[x, z, y, self.core]
            return carry

        lax.fori_loop(0, 16, fold, 0)
        for p, (lo, hi, (d, _, _)) in enumerate(PARTS[self.layer]):
            tail = (pl.ds(lo, hi - lo), slice(None))
            for k in range(4):
                self.kept[p, k] = sub(self.core_buf, {d: (self.at[d] + k) % 4}, tail)
            ra, rb = self.bufs[p][:2]
            self.one[p, 0] = self.step("one", p, 0, self.kept[p, 2].at[HALVES[0]], ra, d, 1)
            self.one[p, 1] = self.step("one", p, 1, self.kept[p, 2].at[HALVES[1]], rb, d, 3)
        for p, (lo, hi, (d, _, _)) in enumerate(PARTS[self.layer]):
            rp, rm = self.bufs[p][2:4]
            self.one[p, 2] = self.step(
                "one", p, 2, self.kept[p, 1].at[HALVES[1]], rp.at[HALVES[1]], d, 1)
            self.one[p, 3] = self.step(
                "one", p, 3, self.kept[p, 3].at[HALVES[0]], rm.at[HALVES[0]], d, 3)

    def middle(self):
        for p, (lo, hi, (d, _, _)) in enumerate(PARTS[self.layer]):
            ra, rb, rp, rm = self.bufs[p][:4]
            self.one[p, 0].wait_recv()
            up = self.kept[p, 1].at[HALVES[0]]
            up[...] = up[...] + ra[...]
            self.one[p, 4] = self.step("one", p, 4, up, rp.at[HALVES[0]], d, 1)
            self.one[p, 1].wait_recv()
            down = self.kept[p, 3].at[HALVES[1]]
            down[...] = down[...] + rb[...]
            self.one[p, 5] = self.step("one", p, 5, down, rm.at[HALVES[1]], d, 3)

    def second(self):
        f32 = jnp.float32
        for p, (lo, hi, (d, e, f)) in enumerate(PARTS[self.layer]):
            rp, rm, r2 = self.bufs[p][2:5]
            for n in range(2, 6):
                self.one[p, n].wait_recv()
            total = self.kept[p, 0]
            for i in range(4):
                total[i] = (total[i].astype(f32) + rp[i].astype(f32) + rm[i].astype(f32)).astype(jnp.bfloat16)
            for k in (2, 1, 3):
                self.two[p, k] = self.step(
                    "two", p, k - 1, self.pick(p, {e: (self.at[e] + k) % 4}), r2.at[k - 1], e, k)

    def pick(self, p, chosen):
        d = PARTS[self.layer][p][2][0]
        return self.kept[p, 0].at[tuple(chosen.get(i, slice(None)) for i in range(3) if i != d)]

    def third(self):
        f32 = jnp.float32
        self.held = {}
        for p, (lo, hi, (d, e, f)) in enumerate(PARTS[self.layer]):
            r2, r3 = self.bufs[p][4:6]
            for k in (1, 2, 3):
                self.two[p, k].wait_recv()
            mine = self.pick(p, {e: self.at[e]})
            mine[...] = (mine[...].astype(f32) + r2[0].astype(f32) + r2[1].astype(f32)
                         + r2[2].astype(f32)).astype(jnp.bfloat16)
            self.held[p] = mine
            for k in (2, 1, 3):
                self.three[p, k] = self.step(
                    "three", p, k - 1, mine.at[(self.at[f] + k) % 4], r3.at[k - 1], f, k)

    def last(self, out_ref):
        f32 = jnp.float32
        for p, (lo, hi, (d, e, f)) in enumerate(PARTS[self.layer]):
            r3 = self.bufs[p][5]
            for k in (1, 2, 3):
                self.three[p, k].wait_recv()
            out_ref[self.layer, pl.ds(lo, hi - lo), :] = (
                self.held[p].at[self.at[f]][...].astype(f32) + r3[0].astype(f32) + r3[1].astype(f32)
                + r3[2].astype(f32))


SEMS = (("core_send", (2,)), ("core_recv", (2,)), ("one_send", (2, 3, 6)), ("one_recv", (2, 3, 6)),
        ("two_send", (2, 3, 3)), ("two_recv", (2, 3, 3)), ("three_send", (2, 3, 3)), ("three_recv", (2, 3, 3)),
        ("fwd_send", ()), ("fwd_recv", ()), ("sum_send", ()), ("sum_recv", ()), ("back_send", ()),
        ("back_recv", ()), ("local", (13,)))


def whole_kernel(slot_ref, block_ref, x_ref, dense_hbm, label_ref, weight_ref, wide_hbm, mid_hbm, narrow_hbm,
                 in_hbm, out_hbm, bias_hbm, head_hbm, sums_ref, back_ref, total_ref,
                 dense_ref, wide_ref, mid_ref, narrow_ref, bias_in, head_ref, slots_ref, w_ref, t_ref, in_ref, out_ref, in_t, out_t, vec_ref, col, cols_ref, sg_ref, lg_ref, start, layer,
                 low0, low1, gate0, gate1, stage, bias_ref, owner_mask, place_mask, close, *rest):
    low = jnp.bfloat16
    f32 = jnp.float32
    projections = (wide_ref, mid_ref, narrow_ref)
    grads, core_bufs, rest = rest[:2], rest[2:4], rest[4:]
    rs_bufs = [[rest[(l * 3 + p) * 6:(l * 3 + p + 1) * 6] for p in range(3)] for l in range(2)]
    sems = {name: sem for (name, _), sem in zip(SEMS, rest[36:-1])}
    sems["round"] = rest[-1]
    at = place()
    me = flat(at)
    sent = []

    def remote(src, dst, ss, rs, to, keep):
        copy = pltpu.make_async_remote_copy(
            src_ref=src, dst_ref=dst, send_sem=ss, recv_sem=rs, device_id=to, device_id_type=MESH)
        copy.start()
        if keep:
            sent.append(copy)
        return copy

    barrier = pltpu.get_barrier_semaphore()

    lines = [[tuple((a + k) % 4 if i == d else a for i, a in enumerate(at[:3])) + at[3:] for k in (1, 2, 3)]
             for d in range(3)]
    near = [at[:3] + (1 - at[3],)] + lines[0] + lines[1] + lines[2]
    for device in near:
        pl.semaphore_signal(barrier, inc=1, device_id=device, device_id_type=MESH)
    loads = []
    for l in range(2):
        loads.append(pltpu.make_async_copy(in_hbm.at[l], in_ref.at[l], sems["local"].at[l]))
        loads.append(pltpu.make_async_copy(out_hbm.at[l], out_ref.at[l], sems["local"].at[2 + l]))
    small_loads = [
        pltpu.make_async_copy(src, dst, sems["local"].at[7 + n]) for n, (src, dst) in enumerate((
            (dense_hbm, dense_ref), (wide_hbm, wide_ref), (mid_hbm, mid_ref), (narrow_hbm, narrow_ref),
            (bias_hbm, bias_in), (head_hbm, head_ref)))]
    for load in small_loads + loads:
        load.start()
    own = pltpu.make_async_copy(x_ref.at[:, columns(me)], slots_ref.at[me], sems["local"].at[4])
    own.start()
    local_sum = jnp.sum(weight_ref[...], axis=1, keepdims=True)
    w_ref[...] = jnp.broadcast_to(local_sum, (1, 128))
    t_ref[me] = jnp.broadcast_to(local_sum, (1, 128))
    ys = [(at[2] + q) % 4 for q in range(4)]
    cores = [at[3], 1 - at[3]]
    xs_now = [(at[0] + q) % 4 for q in range(4)]
    zs_now = [(at[1] + q) % 4 for q in range(4)]

    def to_all(lo, hi, send):
        def some(i, carry):
            xs = [(at[0] + i + q) % 4 for q in range(4)]
            zs = [(at[1] + i // 4 + q) % 4 for q in range(4)]
            for n in range(8):
                to = (xs[TURN_X[n]], zs[TURN_Z[n]], ys[n // 2], cores[n % 2])
                if n == 0:
                    @pl.when(i > 0)
                    def _():
                        send(to)
                else:
                    send(to)
            return carry

        lax.fori_loop(lo, hi, some, 0)

    def send_forward(to):
        remote(x_ref.at[:, columns(flat(to))], slots_ref.at[me], sems["fwd_send"], sems["fwd_recv"], to, False)

    def send_sum(to):
        remote(w_ref, t_ref.at[me], sems["sum_send"], sems["sum_recv"], to, False)

    def send_back(to):
        remote(sg_ref.at[flat(to)], back_ref.at[:, columns(me)], sems["back_send"], sems["back_recv"], to, False)

    def to_known(rounds):
        for x, z, y, c in FORWARD[rounds]:
            send_forward((xs_now[x], zs_now[z], ys[y], cores[c]))

    pl.semaphore_wait(barrier, len(near))
    for d in (2, 1, 0):
        for device in lines[d]:
            pl.semaphore_signal(sems["round"].at[d], inc=1, device_id=device, device_id_type=MESH)
        to_known(2 - d)
        pl.semaphore_wait(sems["round"].at[d], 3)
    to_known(3)


    row = lax.broadcasted_iota(jnp.int32, (TILE, 128), 0)
    lane = lax.broadcasted_iota(jnp.int32, (TILE, 128), 1)
    place_mask[...] = jnp.where(row % SHARE == lane, 1.0, 0.0)
    owner_row = lax.broadcasted_iota(jnp.int32, (OWNERS, TILE), 0)
    owner_lane = lax.broadcasted_iota(jnp.int32, (OWNERS, TILE), 1)
    owner_mask[...] = jnp.where(owner_lane // SHARE == owner_row, 1.0, 0.0).astype(low)
    for g in range(4):
        stage[g, pl.ds(TILE, 8), :] = jnp.zeros((8, 128), f32)
    for load in small_loads:
        load.wait()
    vec_ref[...] = jnp.zeros(vec_ref.shape, f32)
    vec_ref[pl.ds(0, 2), :] = bias_in[...]
    for i in range(WIDTH // 128):
        vec_ref[2, pl.ds(i * 128, 128)] = head_ref[pl.ds(i * 128, 128)]
    for i in range(WIDTH // 128):
        col[pl.ds(i * 128, 128), :] = vec_ref[:, pl.ds(i * 128, 128)].T
    start[pl.ds(0, 128), :] = dense_ref[...]
    for load in loads:
        load.wait()
    for l in range(2):
        in_t[l] = in_ref[l].T
        out_t[l] = out_ref[l].T
    to_all(0, 16, send_sum)
    own.wait()
    most = slots_ref.at[pl.ds(0, DEVICES - 1)]
    pltpu.make_async_copy(most, most, sems["fwd_recv"]).wait()

    def gather(b, carry):
        cols_ref[pl.ds(pl.multiple_of(b * 16, 16), 16), :] = slots_ref[slot_ref[b]]
        return carry

    lax.fori_loop(0, BLOCKS, gather, 0, unroll=8)
    for n, (which, t, column, width) in enumerate(table_rows()):
        start[pl.ds(128 + n * 128, 128), :] = contract(
            projections[which][t], cols_ref[pl.ds(column, width), :], 0, 0).astype(low)

    hidden0 = contract(in_t[0], start[...], 1, 0).astype(low)

    def tile(i):
        return pl.ds(pl.multiple_of(i * TILE, 16), TILE)

    def forward0(i, carry):
        here = tile(i)
        gate = contract(out_t[0, here, :], hidden0, 1, 0) + col[here, 0:1]
        gate0[here, :] = gate
        s = start[here, :].astype(f32)
        layer[here, :] = (s * gate + s).astype(low)
        return carry

    lax.fori_loop(0, TILES, forward0, 0, unroll=4)
    hidden1 = contract(in_t[1], layer[...], 1, 0).astype(low)

    def forward1(i, logit):
        here = tile(i)
        gate = contract(out_t[1, here, :], hidden1, 1, 0) + col[here, 1:2]
        gate1[here, :] = gate
        last = (start[here, :].astype(f32) * gate + layer[here, :].astype(f32)).astype(low).astype(f32)
        return logit + jnp.sum((col[here, 2:3] * last).reshape(TILE // 8, 8, ROWS), axis=0)

    logit = lax.fori_loop(0, TILES, forward1, jnp.zeros((8, ROWS), f32), unroll=8)
    logit = jnp.sum(logit, axis=0, keepdims=True)
    signal = weight_ref[...] * (jax.nn.sigmoid(logit) - label_ref[...].astype(f32))

    def keep_bias(l, i, gate_grad):
        sums = jnp.sum(gate_grad, axis=1, keepdims=True)
        spread = (place_mask[...] * sums).astype(low)
        bias_ref[l, pl.ds(pl.multiple_of(i * OWNERS, 16), OWNERS), :] = contract(owner_mask[...], spread, 1, 0)

    def backward1(i, carry):
        here = tile(i)
        gate_grad = start[here, :].astype(f32) * (col[here, 2:3] * signal)
        keep_bias(1, i, gate_grad)
        low1[here, :] = gate_grad.astype(low)
        return carry

    lax.fori_loop(0, TILES, backward1, 0, unroll=8)
    grad1 = contract(out_ref[1], low1[...], 1, 0).astype(low)
    bias_row = lax.broadcasted_iota(jnp.int32, (SLOT, 128), 0) == SHARE
    reductions = [
        Reduction(l, at, grads[l], core_bufs[l], rs_bufs[l], sems, remote) for l in range(2)]

    def pack(l, i, in_term, out_term):
        for h in range(2):
            stage[h, pl.ds(0, TILE), :] = in_term[:, h * 128:(h + 1) * 128]
            stage[2 + h, pl.ds(0, TILE), :] = out_term[:, h * 128:(h + 1) * 128]
        for o in range(OWNERS):
            block = (i // 2, 2 * (i % 2) + o // 8, (o // 2) % 4, o % 2)
            if l == 0:
                for g in range(4):
                    close[o % 4, pl.ds(SHARE * g, SLOT), :] = stage[g, pl.ds(SHARE * o, SLOT), :]
                close[o % 4, pl.ds(4 * SHARE, 1), :] = bias_ref[l, pl.ds(i * OWNERS + o, 1), :]
                grads[l][block] = close[o % 4, pl.ds(0, CLOSE), :].astype(low)
                continue
            for g in range(4):
                piece = stage[g, pl.ds(SHARE * o, SLOT), :]
                if g == 0:
                    piece = jnp.where(bias_row, bias_ref[l, pl.ds(i * OWNERS + o, 1), :], piece)
                grads[l][block + (pl.ds(g * SLOT, SLOT), slice(None))] = (
                    piece.astype(low))

        @pl.when(i > 0)
        def _():
            reductions[l].send_tile(i - 1)

    def terms1(i, carry):
        here = tile(i)
        pack(1, i, contract(layer[here, :], grad1, 1, 1), contract(low1[here, :], hidden1, 1, 1))
        return carry

    lax.fori_loop(0, TILES, terms1, 0, unroll=4)
    reductions[1].send_tile(TILES - 1)
    reductions[1].first()

    def backward0(i, carry):
        here = tile(i)
        above = col[here, 2:3] * signal
        upstream = above + contract(in_ref[1, here, :], grad1, 1, 0)
        gate_grad = start[here, :].astype(f32) * upstream
        keep_bias(0, i, gate_grad)
        low0[here, :] = gate_grad.astype(low)
        gate0[here, :] = gate1[here, :] * above + gate0[here, :] * upstream + upstream
        return carry

    lax.fori_loop(0, TILES, backward0, 0, unroll=4)
    grad0 = contract(out_ref[0], low0[...], 1, 0).astype(low)
    reductions[1].middle()

    def finish(i, carry):
        here = tile(i)
        low1[here, :] = (gate0[here, :] + contract(in_ref[0, here, :], grad0, 1, 0)).astype(low)
        return carry

    lax.fori_loop(0, TILES, finish, 0, unroll=4)
    for n, (which, t, column, width) in enumerate(table_rows()):
        lg_ref[pl.ds(column // 16, width // 16)] = contract(
            projections[which][t], low1[pl.ds(128 + n * 128, 128), :], 1, 0).astype(low).reshape(
                width // 16, 16, ROWS)

    def spread(s, carry):
        sg_ref[s] = lg_ref[block_ref[s]]
        return carry

    lax.fori_loop(0, BLOCKS, spread, 0, unroll=8)

    own_back = pltpu.make_async_copy(sg_ref.at[me], back_ref.at[:, columns(me)], sems["local"].at[5])
    own_back.start()
    def terms0(i, carry):
        here = tile(i)
        pack(0, i, contract(start[here, :], grad0, 1, 1), contract(low0[here, :], hidden0, 1, 1))
        return carry

    to_all(0, 5, send_back)
    lax.fori_loop(0, TILES, terms0, 0, unroll=4)
    reductions[0].send_tile(TILES - 1)
    reductions[1].second()
    to_all(5, 7, send_back)
    reductions[0].first()
    reductions[1].third()
    to_all(7, 10, send_back)
    reductions[0].middle()
    reductions[1].last(sums_ref)
    to_all(10, 13, send_back)
    reductions[0].second()
    to_all(13, 16, send_back)
    small = t_ref.at[pl.ds(0, DEVICES - 1)]
    pltpu.make_async_copy(small, small, sems["sum_recv"]).wait()
    total_ref[...] = jnp.sum(t_ref[...], axis=0)
    reductions[0].third()
    reductions[0].last(sums_ref)

    own_back.wait()
    for copy in sent:
        copy.wait_send()
    for reduction in reductions:
        reduction.wait_core("core_send")
    pltpu.make_async_copy(small, small, sems["sum_send"]).wait()
    pltpu.make_async_copy(most, most, sems["fwd_send"]).wait()
    pltpu.make_async_copy(most, most, sems["back_send"]).wait()
    pltpu.make_async_copy(most, most, sems["back_recv"]).wait()


def whole(slot_of_block, block_of_slot, pooled, dense, labels, weights, wide, mid, narrow, cross_in, cross_out, bias,
          head):
    vmem = pl.BlockSpec(memory_space=VM)
    smem = pl.BlockSpec(memory_space=pltpu.SMEM)
    hbm = pl.BlockSpec(memory_space=pl.ANY)
    low, f32 = jnp.bfloat16, jnp.float32
    activation = VM((WIDTH, ROWS), low)
    full = VM((WIDTH, ROWS), f32)
    scratch = [
        VM((128, ROWS), low), VM(wide.shape, low), VM(mid.shape, low), VM(narrow.shape, low), VM(bias.shape, f32),
        VM(head.shape, f32),
        VM((DEVICES, 16, ROWS), low), VM((1, 128), f32), VM((DEVICES, 1, 128), f32),
        VM((2, WIDTH, 256), low), VM((2, 256, WIDTH), low), VM((2, 256, WIDTH), low), VM((2, WIDTH, 256), low),
        VM((8, WIDTH), f32), VM((WIDTH, 8), f32), VM((2048, ROWS), low), VM((DEVICES, 16, ROWS), low),
        VM((DEVICES, 16, ROWS), low),
        activation, activation, activation, activation, full, full,
        VM((4, TILE + 8, 128), f32), VM((2, DEVICES, 128), f32), VM((OWNERS, TILE), low), VM((TILE, 128), f32),
        VM((4, 120, 128), f32),
    ]
    scratch += [VM((4, 4, 4, 2, n, 128), low) for n in (CLOSE, OWNED)]
    scratch += [VM((4, 4, 4, n, 128), low) for n in (CLOSE, OWNED)]
    for l in range(2):
        for lo, hi, _ in PARTS[l]:
            n = hi - lo
            scratch += [VM((2, 4, n, 128), low), VM((2, 4, n, 128), low), VM((4, 4, n, 128), low),
                        VM((4, 4, n, 128), low), VM((3, 4, n, 128), low), VM((3, n, 128), low)]
    scratch += [pltpu.SemaphoreType.DMA(shape) if shape else pltpu.SemaphoreType.DMA for _, shape in SEMS]
    scratch.append(pltpu.SemaphoreType.REGULAR((3,)))
    return pl.pallas_call(
        whole_kernel,
        out_shape=(jax.ShapeDtypeStruct((2, OWNED, 128), f32),
                   jax.ShapeDtypeStruct((16, DEVICES * ROWS), low),
                   jax.ShapeDtypeStruct((1, 128), f32)),
        in_specs=[smem, smem, hbm, hbm, vmem, vmem] + [hbm] * 7,
        out_specs=(vmem, vmem, vmem),
        scratch_shapes=scratch,
        compiler_params=pltpu.CompilerParams(
            has_side_effects=True, collective_id=0, vmem_limit_bytes=60 * 1024 * 1024),
        name="whole",
    )(slot_of_block, block_of_slot, pooled, dense, labels, weights, wide, mid, narrow, cross_in, cross_out, bias, head)


PIECES = 2


def post_kernel(back_ref, sums_ref, total_ref, pooled_ref, in_ref, out_ref, bias_ref):
    scale = BATCH_ROWS / total_ref[...]
    many = back_ref.shape[1] // 128

    def move(j, carry):
        part = back_ref[:, pl.ds(pl.multiple_of(j * 1024, 1024), 1024)].astype(jnp.float32) * wide
        pooled_ref[:, pl.ds(pl.multiple_of(j * 8, 8), 8), :] = pltpu.einshape("c(jl)->cjl", part, j=8, l=128)
        return carry

    wide = jnp.tile(scale, (1, 8))
    lax.fori_loop(0, many // 8, move, 0, unroll=2)

    @pl.when(pl.program_id(0) == 0)
    def _():
        for l in range(2):
            for h in range(2):
                step = (SHARE, SLOT)[l]
                in_ref[:, h, l, :] = sums_ref[l, pl.ds(h * step, SHARE), :] * scale
                out_ref[:, h, l, :] = sums_ref[l, pl.ds((2 + h) * step, SHARE), :] * scale
            bias_ref[pl.ds(l, 1), :] = (sums_ref[l, pl.ds((4 * SHARE, SHARE)[l], 1), :] * scale)[:, :SHARE]


def post(returned, sums, total):
    f32 = jnp.float32
    many = DEVICES * ROWS // 128
    once = lambda shape: pl.BlockSpec(shape, lambda i: (0,) * len(shape))
    return pl.pallas_call(
        post_kernel,
        grid=(PIECES,),
        out_shape=(jax.ShapeDtypeStruct((BLOCK_WIDTH, many, 128), f32),
                   jax.ShapeDtypeStruct((SHARE, 2, 2, 128), f32),
                   jax.ShapeDtypeStruct((SHARE, 2, 2, 128), f32),
                   jax.ShapeDtypeStruct((2, SHARE), f32)),
        in_specs=[pl.BlockSpec((BLOCK_WIDTH, DEVICES * ROWS // PIECES), lambda i: (0, i)),
                  once((2, OWNED, 128)), once((1, 128))],
        out_specs=(pl.BlockSpec((BLOCK_WIDTH, many // PIECES, 128), lambda i: (0, i, 0)),
                   once((SHARE, 2, 2, 128)), once((SHARE, 2, 2, 128)), once((2, SHARE))),
        name="post",
    )(returned, sums, total)


def unpacked(rows):
    return jnp.transpose(rows, (2, 0, 1, 3)).reshape(2, SHARE, 256)


def body(
    pooled,
    slot_of_block,
    dense_part,
    labels,
    sample_weight,
    proj_wide,
    proj_mid,
    proj_narrow,
    cross_in,
    cross_out,
    cross_bias,
    head_weight,
):
    numbers = jnp.arange(BLOCKS, dtype=jnp.int32)
    block_of_slot = jnp.max(jnp.where(slot_of_block[None, :] == numbers[:, None], numbers[None, :], 0), 1)
    sums, returned, total = whole(
        slot_of_block,
        block_of_slot,
        pooled.reshape(BLOCK_WIDTH, BATCH_ROWS),
        dense_part,
        labels[None],
        sample_weight[None],
        proj_wide,
        proj_mid,
        proj_narrow,
        cross_in,
        cross_out,
        cross_bias,
        head_weight,
    )
    pooled_grad, grad_in, grad_out, grad_bias = post(returned, sums, total)
    return (
        pooled_grad.reshape(BLOCK_WIDTH, 1, BATCH_ROWS),
        unpacked(grad_in),
        jnp.swapaxes(unpacked(grad_out), 1, 2),
        grad_bias,
    )


def solution(mesh):
    finer = Mesh(mesh.devices.reshape(4, 4, 4, mesh.shape["rep"]), ("dp_0", "dp_1", "dp_2", "rep"))
    return jax.shard_map(
        body,
        mesh=finer,
        in_specs=(
            P(None, DP_REP, None),
            P(),
            P(None, DP_REP),
            P(DP_REP),
            P(DP_REP),
            P(),
            P(),
            P(),
            P(),
            P(),
            P(),
            P(),
        ),
        out_specs=(
            P(None, DP_REP, None),
            P(None, DP_REP, None),
            P(None, None, DP_REP),
            P(None, DP_REP),
        ),
        check_vma=False,
    )
```
